256 devices in a mesh: blk: 64 (over y, x, z_hi, core), grp: 4 (over z_lo).
Axes of the slice: x: 4, y: 4, z: 8 (z_hi: 2, z_lo: 4; z = z_hi * 4 + z_lo), core: 2. Of those that a mesh axis runs over, the one named last changes fastest.
Arguments:
- amplitudes: float32 [2048, 4, 65536], P('grp', None, 'blk'), may hold values from -6 to 6
- integrals: float32 [4, 65536, 256], P('grp', 'blk'), may hold values from -0.0234375 to 0.0234375
- irrep_sizes: int32 [4], replicated, may hold values from 86 to 256, as said below
- owner_map: int32 [4], replicated, may hold values from 0 to 3, each once
Outputs:
- ladder: float32 [2048, 4, 256], P('grp', None, 'blk')
The draws below stay inside these ranges and needn't reach their ends.
Inputs may be any that keep to these rules, and one draw needn't show every extreme that they name: `irrep_sizes`: one irrep fills its block and one has the smallest size.
All inputs are finite; a program needn't handle non-finite values.
Results may differ from the reference program's by a relative error of at most 0.0001.
Values sent between devices are 32-bit elements; how exact they have to be, the bound alone decides.
No kernel may reach another device: no remote copies, remote signals or barrier semaphores. Data moves between devices by JAX's collectives and lax.ppermute only.
A program may use at most 128 MiB of HBM per device.

```python
import jax
import jax.numpy as jnp
from jax import lax

BLOCK = 256
IRREPS = 4
AB_W = 256
SLOTS = 65536
PAIRS = 2048


def draw_irrep_sizes(key, part):
    first_key, second_key = jax.random.split(jax.random.fold_in(key, 11))
    lowest = (BLOCK + 2) // 3
    sizes = jax.random.randint(first_key, (IRREPS,), lowest, BLOCK + 1)
    order = jax.random.permutation(second_key, IRREPS)
    places = jnp.arange(IRREPS)
    sizes = jnp.where(places == order[0], BLOCK, sizes)
    sizes = jnp.where(places == order[1], lowest, sizes)
    return sizes.astype(jnp.int32)


def block_levels(stream_key, shape, cuts, smallest, top_value):
    gain = 1.0
    for dim, parts in cuts:
        draws = jax.random.uniform(jax.random.fold_in(jax.random.fold_in(stream_key, 6), dim), (parts,), jnp.float32, smallest / len(cuts), top_value / len(cuts))
        gain = gain * jnp.repeat(jnp.exp(draws), shape[dim] // parts).reshape((-1,) + (1,) * (len(shape) - 1 - dim))
    return gain


def bell_draw(key, extent, scale, reach, pieces=(), kind=jnp.bfloat16):
    entries = scale * jax.random.normal(key, extent, jnp.float32)
    if pieces:
        entries = entries * block_levels(key, extent, pieces, -0.22, 0.18)
    return jnp.clip(entries, -reach, reach).astype(kind)


def setup_inputs(seed: int = 0) -> dict:
    key_list = jax.random.split(jax.random.key(seed), 5)
    amplitudes = bell_draw(key_list[0], (PAIRS, IRREPS, SLOTS), 1.0, 6.0, ((0, 4), (2, 64)), jnp.float32)
    integrals = bell_draw(key_list[1], (IRREPS, SLOTS, AB_W), SLOTS ** -0.5, 0.0234375, ((0, 4), (1, 64)), jnp.float32)
    irrep_sizes = draw_irrep_sizes(jax.random.fold_in(key_list[4], 71), 0)
    owner_map = jax.random.permutation(key_list[3], IRREPS).astype(jnp.int32)
    return {"amplitudes": amplitudes, "integrals": integrals, "irrep_sizes": irrep_sizes, "owner_map": owner_map}


def slot_valid(irrep_sizes, offset, width):
    slot = offset + jnp.arange(width, dtype=jnp.int32)
    sizes = irrep_sizes.astype(jnp.int32)[:, None]
    return ((slot[None, :] // BLOCK < sizes) & (slot[None, :] % BLOCK < sizes)).astype(jnp.float32)


def reference(amplitudes, integrals, irrep_sizes, owner_map):
    row_valid = slot_valid(irrep_sizes, 0, SLOTS)
    column_valid = slot_valid(irrep_sizes, 0, AB_W)
    masked = amplitudes * row_valid[None, :, :]
    blocks = []
    for irrep in range(IRREPS):
        slab_rows = lax.dynamic_index_in_dim(integrals, owner_map[irrep].astype(jnp.int32), 0, keepdims=False)
        blocks.append(jnp.dot(masked[:, irrep, :], slab_rows, precision=lax.Precision.HIGHEST, preferred_element_type=jnp.float32))
    result = jnp.stack(blocks, axis=1)
    return result * column_valid[None, :, :]
```

```python
import jax
import jax.numpy as jnp
from jax import lax
from jax.sharding import PartitionSpec as P

BLOCK = 256
IRREPS = 4
NY, NX, NZ, NC, NG = 4, 4, 2, 2, 4
AXES = ("blk", "grp")


def blk_index(y, x, z, c):
    return ((y * NX + x) * NZ + z) * NC + c


def every_device():
    for y in range(NY):
        for x in range(NX):
            for z in range(NZ):
                for c in range(NC):
                    for g in range(NG):
                        yield y, x, z, c, g


def permute(value, target):
    pairs = []
    for place in every_device():
        there = target(*place)
        pairs.append((blk_index(*place[:4]) * NG + place[4], blk_index(*there[:4]) * NG + there[4]))
    return lax.ppermute(value, AXES, pairs)


def plane_groups():
    return [[blk_index(y, x, z, c) for y in range(NY) for x in range(NX)] for z in range(NZ) for c in range(NC)]


RELAY = {1: 0, 0: 2, 2: 3, 3: 1}


def slot_valid(irrep_sizes, offset, width):
    slot = offset + jnp.arange(width, dtype=jnp.int32)
    sizes = irrep_sizes[:, None]
    return ((slot[None, :] // BLOCK < sizes) & (slot[None, :] % BLOCK < sizes)).astype(jnp.float32)


def local(amplitudes, integrals, irrep_sizes, owner_map):
    pairs, _, slot_width = amplitudes.shape
    columns = integrals.shape[2]
    column_width = columns // lax.axis_size("blk")
    half = pairs // 2
    position = lax.axis_index("blk")
    group = lax.axis_index("grp")
    core = position % NC
    z_part = (position // NC) % NZ

    own = integrals[0]
    one = permute(own, lambda y, x, z, c, g: (y, x, z, c, g ^ 1))
    two = permute(own, lambda y, x, z, c, g: (y, x, z, c, g ^ 2))
    relayed = jnp.where((group == 0) | (group == 3), one, two)
    three = permute(relayed, lambda y, x, z, c, g: (y, x, z, c, RELAY[g]))

    row_valid = slot_valid(irrep_sizes, position * slot_width, slot_width)
    irrep_of = jnp.argsort(owner_map)

    def reduced(slot, slab):
        irrep = irrep_of[group ^ slot]
        chosen = lax.dynamic_index_in_dim(amplitudes, irrep, 1, keepdims=False)
        chosen = chosen * lax.dynamic_index_in_dim(row_valid, irrep, 0, keepdims=True)
        mine = lax.dynamic_slice_in_dim(chosen, core * half, half, 0)
        other = lax.dynamic_slice_in_dim(chosen, (1 - core) * half, half, 0)

        def product(rows):
            return lax.dot_general(
                slab, rows, (((0,), (1,)), ((), ())), precision=lax.Precision.HIGH, preferred_element_type=jnp.float32
            )

        sent = permute(product(other), lambda y, x, z, c, g: (y, x, z, 1 - c, g))
        chip = product(mine) + sent
        chip = chip.reshape(NY * NX, columns // (NY * NX), half)
        spread = lax.all_to_all(chip, "blk", 0, 0, tiled=True, axis_index_groups=plane_groups())
        return jnp.sum(spread, axis=0)

    parts = jnp.stack([reduced(slot, slab) for slot, slab in enumerate((own, one, two, three))])
    parts = parts.reshape(IRREPS, NZ, NC * column_width, half)
    kept = lax.dynamic_index_in_dim(parts, z_part, 1, keepdims=False)
    sent = lax.dynamic_index_in_dim(parts, 1 - z_part, 1, keepdims=False)
    parts = kept + permute(sent, lambda y, x, z, c, g: (y, x, 1 - z, c, g))
    parts = parts.reshape(IRREPS, NC, column_width, half)
    kept = lax.dynamic_index_in_dim(parts, core, 1, keepdims=False)
    sent = lax.dynamic_index_in_dim(parts, 1 - core, 1, keepdims=False)
    got = permute(sent, lambda y, x, z, c, g: (y, x, z, 1 - c, g))
    first = core == 0
    whole = jnp.concatenate([jnp.where(first, kept, got), jnp.where(first, got, kept)], axis=2)
    result = whole[owner_map ^ group]
    column_valid = slot_valid(irrep_sizes, position * column_width, column_width)
    return jnp.transpose(result * column_valid[:, :, None], (2, 0, 1))


def solution(mesh):
    in_specs = (P("grp", None, "blk"), P("grp", "blk", None), P(), P())
    out_specs = P("grp", None, "blk")
    return jax.shard_map(local, mesh=mesh, in_specs=in_specs, out_specs=out_specs, check_vma=False)
```

```python
import functools

import jax
import jax.numpy as jnp
from jax import lax
from jax.experimental import pallas as pl
from jax.experimental.pallas import tpu as pltpu
from jax.sharding import PartitionSpec as P

BLOCK = 256
IRREPS = 4
LANES = 128
NY, NX, NZ, NC, NG = 4, 4, 2, 2, 4
AXES = ("blk", "grp")


def blk_index(y, x, z, c):
    return ((y * NX + x) * NZ + z) * NC + c


def every_device():
    for y in range(NY):
        for x in range(NX):
            for z in range(NZ):
                for c in range(NC):
                    for g in range(NG):
                        yield y, x, z, c, g


def permute(value, target):
    pairs = []
    for place in every_device():
        there = target(*place)
        pairs.append((blk_index(*place[:4]) * NG + place[4], blk_index(*there[:4]) * NG + there[4]))
    return lax.ppermute(value, AXES, pairs)


def plane_groups():
    return [[blk_index(y, x, z, c) for y in range(NY) for x in range(NX)] for z in range(NZ) for c in range(NC)]


RELAY = {1: 0, 0: 2, 2: 3, 3: 1}


def slot_valid(irrep_sizes, offset, width):
    slot = offset + jnp.arange(width, dtype=jnp.int32)
    sizes = irrep_sizes[:, None]
    return ((slot[None, :] // BLOCK < sizes) & (slot[None, :] % BLOCK < sizes)).astype(jnp.float32)


def split_kernel(rows, slot_width, scalars, source, *outputs):
    tiles = slot_width // LANES
    group, position = scalars[2 * IRREPS], scalars[2 * IRREPS + 1]
    lane = lax.broadcasted_iota(jnp.int32, (rows, LANES), 1)
    for slot in range(IRREPS):
        irrep = jnp.int32(0)
        for h in range(IRREPS):
            irrep = jnp.where(scalars[h] == (group ^ slot), h, irrep)
        size = scalars[IRREPS + irrep]
        high, low = outputs[2 * slot], outputs[2 * slot + 1]
        for tile in range(tiles):
            first = position * slot_width + tile * LANES
            limit = jnp.where(first // BLOCK < size, size - first % BLOCK, 0)
            value = source[pl.ds(tile * IRREPS + irrep, rows, stride=tiles * IRREPS), :]
            value = jnp.where(lane < limit, value, 0.0)
            rounded = value.astype(jnp.bfloat16)
            place = slice(tile * LANES, (tile + 1) * LANES)
            high[0, :, place] = rounded
            low[0, :, place] = (value - rounded.astype(jnp.float32)).astype(jnp.bfloat16)


def split_rows(amplitudes, scalars):
    pairs, _, slot_width = amplitudes.shape
    half = pairs // 2
    rows = 64
    steps = half // rows
    view = amplitudes.reshape(pairs, IRREPS, slot_width // LANES, LANES).transpose(0, 2, 1, 3).reshape(-1, LANES)

    def out_index(i, scalars):
        return ((i // steps) ^ scalars[2 * IRREPS + 2] ^ 1, i % steps, 0)

    return pl.pallas_call(
        functools.partial(split_kernel, rows, slot_width),
        out_shape=[jax.ShapeDtypeStruct((2, half, slot_width), jnp.bfloat16)] * (2 * IRREPS),
        grid_spec=pltpu.PrefetchScalarGridSpec(
            num_scalar_prefetch=1,
            grid=(2 * steps,),
            in_specs=[pl.BlockSpec((rows * IRREPS * slot_width // LANES, LANES), lambda i, scalars: (i, 0))],
            out_specs=[pl.BlockSpec((1, rows, slot_width), out_index)] * (2 * IRREPS),
        ),
        compiler_params=pltpu.CompilerParams(vmem_limit_bytes=16 << 20),
        cost_estimate=pl.CostEstimate(flops=0, bytes_accessed=8 * pairs * IRREPS * slot_width, transcendentals=0),
        name="split_rows",
    )(scalars, view)


def product_kernel(part, slab, high, low, out):
    value = slab[...]
    rounded = value.astype(jnp.bfloat16)
    rest = (value - rounded.astype(jnp.float32)).astype(jnp.bfloat16)
    dot = functools.partial(jnp.dot, preferred_element_type=jnp.float32)
    total = dot(high[part], rounded) + (dot(high[part], rest) + dot(low[part], rounded))
    out[...] = total.T


def product(slab, high, low, part):
    slots, columns = slab.shape
    half = high.shape[1]
    return pl.pallas_call(
        functools.partial(product_kernel, part),
        out_shape=jax.ShapeDtypeStruct((columns, half), jnp.float32),
        in_specs=[pl.BlockSpec(memory_space=pltpu.VMEM)] * 3,
        out_specs=pl.BlockSpec(memory_space=pltpu.VMEM),
        compiler_params=pltpu.CompilerParams(vmem_limit_bytes=16 << 20),
        cost_estimate=pl.CostEstimate(
            flops=6 * slots * columns * half, bytes_accessed=4 * slots * (columns + half), transcendentals=0
        ),
        name="product",
    )(slab, high, low)


def local(amplitudes, integrals, irrep_sizes, owner_map):
    slot_width = amplitudes.shape[2]
    columns = integrals.shape[2]
    column_width = columns // lax.axis_size("blk")
    half = amplitudes.shape[0] // 2
    position = lax.axis_index("blk")
    group = lax.axis_index("grp")
    core = position % NC
    z_part = (position // NC) % NZ

    own = integrals[0]
    one = permute(own, lambda y, x, z, c, g: (y, x, z, c, g ^ 1))
    two = permute(own, lambda y, x, z, c, g: (y, x, z, c, g ^ 2))

    scalars = jnp.concatenate([owner_map, irrep_sizes, jnp.stack([group, position, core])])
    split = split_rows(amplitudes, scalars)

    def on_chip(slot, slab):
        high, low = split[2 * slot], split[2 * slot + 1]
        sent = permute(product(slab, high, low, 0), lambda y, x, z, c, g: (y, x, z, 1 - c, g))
        chip = product(slab, high, low, 1) + sent
        return chip.reshape(NY * NX, columns // (NY * NX), half)

    def over_plane(chip):
        spread = lax.all_to_all(chip, "blk", 0, 0, tiled=True, axis_index_groups=plane_groups())
        return jnp.sum(spread, axis=0)

    part_own = over_plane(on_chip(0, own))
    one, two, part_own = lax.optimization_barrier((one, two, part_own))
    relayed = jnp.where((group == 0) | (group == 3), one, two)
    three = permute(relayed, lambda y, x, z, c, g: (y, x, z, c, RELAY[g]))
    part_pair = over_plane(jnp.concatenate([on_chip(1, one), on_chip(2, two)], axis=1))
    part_three = over_plane(on_chip(3, three))

    parts = jnp.concatenate([part_own, part_pair, part_three], axis=0)
    parts = parts.reshape(IRREPS, NZ, NC * column_width, half)
    kept = lax.dynamic_index_in_dim(parts, z_part, 1, keepdims=False)
    sent = lax.dynamic_index_in_dim(parts, 1 - z_part, 1, keepdims=False)
    parts = kept + permute(sent, lambda y, x, z, c, g: (y, x, 1 - z, c, g))
    parts = parts.reshape(IRREPS, NC, column_width, half)
    kept = lax.dynamic_index_in_dim(parts, core, 1, keepdims=False)
    sent = lax.dynamic_index_in_dim(parts, 1 - core, 1, keepdims=False)
    got = permute(sent, lambda y, x, z, c, g: (y, x, z, 1 - c, g))
    first = core == 0
    whole = jnp.concatenate([jnp.where(first, kept, got), jnp.where(first, got, kept)], axis=2)
    result = whole[owner_map ^ group]
    column_valid = slot_valid(irrep_sizes, position * column_width, column_width)
    return jnp.transpose(result * column_valid[:, :, None], (2, 0, 1))


def solution(mesh):
    in_specs = (P("grp", None, "blk"), P("grp", "blk", None), P(), P())
    out_specs = P("grp", None, "blk")
    return jax.shard_map(local, mesh=mesh, in_specs=in_specs, out_specs=out_specs, check_vma=False)
```

```python
import functools

import jax
import jax.numpy as jnp
from jax import lax
from jax.experimental import pallas as pl
from jax.experimental.pallas import tpu as pltpu
from jax.sharding import PartitionSpec as P


BLOCK = 256
IRREPS = 4
LANES = 128
NY, NX, NZ, NC, NG = 4, 4, 2, 2, 4
AXES = ("blk", "grp")


def blk_index(y, x, z, c):
    return ((y * NX + x) * NZ + z) * NC + c


def every_device():
    for y in range(NY):
        for x in range(NX):
            for z in range(NZ):
                for c in range(NC):
                    for g in range(NG):
                        yield y, x, z, c, g


def permute(value, target):
    pairs = []
    for place in every_device():
        there = target(*place)
        if there is None:
            continue
        pairs.append((blk_index(*place[:4]) * NG + place[4], blk_index(*there[:4]) * NG + there[4]))
    return lax.ppermute(value, AXES, pairs)


def plane_groups():
    return [[blk_index(y, x, z, c) for y in range(NY) for x in range(NX)] for z in range(NZ) for c in range(NC)]


def plane_sum(chip):
    spread = lax.all_to_all(chip, "blk", 0, 0, tiled=True, axis_index_groups=plane_groups())
    return jnp.sum(spread, axis=0)


def pair_swap(y, x, z, c, g):
    return y, x, z, c, g ^ 1


def middle_swap(y, x, z, c, g):
    return (y, x, z, c, 3 - g) if g in (1, 2) else None


def outward(y, x, z, c, g):
    return (y, x, z, c, {1: 0, 2: 3}[g]) if g in (1, 2) else None


def split_kernel(rows, slot_width, scalars, source, *outputs):
    tiles = slot_width // LANES
    group, position = scalars[2 * IRREPS], scalars[2 * IRREPS + 1]
    lane = lax.broadcasted_iota(jnp.int32, (rows, LANES), 1)
    for slot in range(IRREPS):
        irrep = jnp.int32(0)
        for h in range(IRREPS):
            irrep = jnp.where(scalars[h] == (group ^ slot), h, irrep)
        size = scalars[IRREPS + irrep]
        high, low = outputs[2 * slot], outputs[2 * slot + 1]
        for tile in range(tiles):
            first = position * slot_width + tile * LANES
            limit = jnp.where(first // BLOCK < size, size - first % BLOCK, 0)
            value = source[pl.ds(tile * IRREPS + irrep, rows, stride=tiles * IRREPS), :]
            value = jnp.where(lane < limit, value, 0.0)
            rounded = value.astype(jnp.bfloat16)
            place = slice(tile * LANES, (tile + 1) * LANES)
            high[:, place] = rounded
            low[:, place] = (value - rounded.astype(jnp.float32)).astype(jnp.bfloat16)


def split_rows(amplitudes, scalars):
    pairs, _, slot_width = amplitudes.shape
    rows = 64
    view = amplitudes.reshape(pairs, IRREPS, slot_width // LANES, LANES).transpose(0, 2, 1, 3).reshape(-1, LANES)
    return pl.pallas_call(
        functools.partial(split_kernel, rows, slot_width),
        out_shape=[jax.ShapeDtypeStruct((pairs, slot_width), jnp.bfloat16)] * (2 * IRREPS),
        grid_spec=pltpu.PrefetchScalarGridSpec(
            num_scalar_prefetch=1,
            grid=(pairs // rows,),
            in_specs=[pl.BlockSpec((rows * IRREPS * slot_width // LANES, LANES), lambda i, scalars: (i, 0))],
            out_specs=[pl.BlockSpec((rows, slot_width), lambda i, scalars: (i, 0))] * (2 * IRREPS),
        ),
        compiler_params=pltpu.CompilerParams(vmem_limit_bytes=16 << 20),
        cost_estimate=pl.CostEstimate(flops=0, bytes_accessed=8 * pairs * IRREPS * slot_width, transcendentals=0),
        name="split_rows",
    )(scalars, view)


def product_kernel(alternatives, parts, scalars, *refs):
    slabs, (high, low, out, high_here, low_here, sems) = refs[: alternatives * parts], refs[alternatives * parts :]
    depth = slabs[0].shape[0]
    copies = []
    for part in range(parts):
        place = pl.ds(part * depth, depth)
        for k, (there, here) in enumerate(((high, high_here), (low, low_here))):
            copies.append(pltpu.make_async_copy(there.at[:, place], here.at[:, place], sems.at[part, k]))
            copies[-1].start()
    group = scalars[2 * IRREPS]
    ends = (group == 0) | (group == NG - 1)
    dot = functools.partial(jnp.dot, preferred_element_type=jnp.float32)
    total = None
    for part in range(parts):
        if alternatives == 1:
            value = slabs[part][...]
        else:
            value = jnp.where(ends, slabs[part][...], slabs[parts + part][...])
        rounded = value.astype(jnp.bfloat16)
        rest = (value - rounded.astype(jnp.float32)).astype(jnp.bfloat16)
        copies[2 * part].wait()
        copies[2 * part + 1].wait()
        place = slice(part * depth, (part + 1) * depth)
        high_part, low_part = high_here[:, place], low_here[:, place]
        term = dot(high_part, rounded) + (dot(high_part, rest) + dot(low_part, rounded))
        total = term if total is None else total + term
    out[...] = total.T


def product(scalars, choices, high, low):
    parts = len(choices[0])
    _, columns = choices[0][0].shape
    pairs, slots = high.shape
    vmem = pl.BlockSpec(memory_space=pltpu.VMEM)
    return pl.pallas_call(
        functools.partial(product_kernel, len(choices), parts),
        out_shape=jax.ShapeDtypeStruct((columns, pairs), jnp.float32),
        in_specs=[pl.BlockSpec(memory_space=pltpu.SMEM)]
        + [vmem] * (len(choices) * parts)
        + [pl.BlockSpec(memory_space=pl.ANY)] * 2,
        out_specs=vmem,
        scratch_shapes=[pltpu.VMEM((pairs, slots), jnp.bfloat16)] * 2 + [pltpu.SemaphoreType.DMA((parts, 2))],
        compiler_params=pltpu.CompilerParams(vmem_limit_bytes=16 << 20),
        cost_estimate=pl.CostEstimate(
            flops=6 * slots * columns * pairs, bytes_accessed=4 * slots * (columns + pairs), transcendentals=0
        ),
        name="product",
    )(scalars, *[piece for choice in choices for piece in choice], high, low)


def finish_kernel(column_width, scalars, *refs):
    parts, out = refs[:-1], refs[-1]
    group, position = scalars[2 * IRREPS], scalars[2 * IRREPS + 1]
    column = position * column_width + lax.broadcasted_iota(jnp.int32, out.shape[1:], 0)
    for irrep in range(IRREPS):
        slot = scalars[irrep] ^ group
        size = scalars[IRREPS + irrep]
        total = parts[0][slot]
        for part in parts[1:]:
            total = total + part[slot]
        valid = (column // BLOCK < size) & (column % BLOCK < size)
        out[irrep] = jnp.where(valid, total, 0.0)


def finish(scalars, parts):
    vmem = pl.BlockSpec(memory_space=pltpu.VMEM)
    return pl.pallas_call(
        functools.partial(finish_kernel, parts[0].shape[1]),
        out_shape=jax.ShapeDtypeStruct(parts[0].shape, jnp.float32),
        in_specs=[pl.BlockSpec(memory_space=pltpu.SMEM)] + [vmem] * len(parts),
        out_specs=vmem,
        compiler_params=pltpu.CompilerParams(vmem_limit_bytes=4 << 20),
        name="finish",
    )(scalars, *parts)


def local(amplitudes, integrals, irrep_sizes, owner_map):
    pairs = amplitudes.shape[0]
    rows, columns = integrals.shape[1:]
    column_width = columns // lax.axis_size("blk")
    position = lax.axis_index("blk")
    group = lax.axis_index("grp")
    core = position % NC
    z_part = (position // NC) % NZ

    own = integrals[0]
    halves = [own[: rows // 2], own[rows // 2 :]]
    near, middle = [], []
    for piece in halves:
        near.append(permute(piece, pair_swap))
        middle.append(permute(piece, middle_swap))
    crossed = [permute(piece, middle_swap) for piece in near]
    passed = [permute(piece, outward) for piece in middle]
    far = [permute(piece, outward) for piece in crossed]

    scalars = jnp.concatenate([owner_map, irrep_sizes, jnp.stack([group, position])])
    split = split_rows(amplitudes, scalars)

    def columns_of(slot, *choices):
        result = product(scalars, choices, split[2 * slot], split[2 * slot + 1])
        return result.reshape(NY * NX, columns // (NY * NX), pairs)

    first = plane_sum(jnp.concatenate([columns_of(0, [own]), columns_of(1, near)], axis=1))
    second = plane_sum(columns_of(2, passed, crossed))
    third = plane_sum(columns_of(3, far, middle))
    total = jnp.concatenate([first, second, third], axis=0).reshape(IRREPS, NZ * NC, column_width, pairs)

    def share(flip):
        here = (z_part * NC + core) ^ flip
        return lax.dynamic_index_in_dim(total, here, 1, keepdims=False)

    parts = [share(0)]
    for flip in (3, 2, 1):
        parts.append(permute(share(flip), lambda y, x, z, c, g: (y, x, z ^ (flip >> 1), c ^ (flip & 1), g)))
    return jnp.transpose(finish(scalars, parts), (2, 0, 1))


def solution(mesh):
    in_specs = (P("grp", None, "blk"), P("grp", "blk", None), P(), P())
    out_specs = P("grp", None, "blk")
    return jax.shard_map(local, mesh=mesh, in_specs=in_specs, out_specs=out_specs, check_vma=False)
```

```python
import functools

import jax
import jax.numpy as jnp
from jax import lax
from jax.experimental import pallas as pl
from jax.experimental.pallas import tpu as pltpu
from jax.sharding import PartitionSpec as P


BLOCK = 256
IRREPS = 4
LANES = 128
NY, NX, NZ, NC, NG = 4, 4, 2, 2, 4
AXES = ("blk", "grp")


def blk_index(y, x, z, c):
    return ((y * NX + x) * NZ + z) * NC + c


def every_device():
    for y in range(NY):
        for x in range(NX):
            for z in range(NZ):
                for c in range(NC):
                    for g in range(NG):
                        yield y, x, z, c, g


def permute(value, target):
    pairs = []
    for place in every_device():
        there = target(*place)
        if there is None:
            continue
        pairs.append((blk_index(*place[:4]) * NG + place[4], blk_index(*there[:4]) * NG + there[4]))
    return lax.ppermute(value, AXES, pairs)


def plane_groups():
    return [[blk_index(y, x, z, c) for y in range(NY) for x in range(NX)] for z in range(NZ) for c in range(NC)]


def plane_sum(chip):
    spread = lax.all_to_all(chip, "blk", 0, 0, tiled=True, axis_index_groups=plane_groups())
    return jnp.sum(spread, axis=0)


def pair_swap(y, x, z, c, g):
    return y, x, z, c, g ^ 1


def middle_swap(y, x, z, c, g):
    return (y, x, z, c, 3 - g) if g in (1, 2) else None


def inward(y, x, z, c, g):
    return (y, x, z, c, {0: 1, 3: 2}[g]) if g in (0, 3) else None


def outward(y, x, z, c, g):
    return (y, x, z, c, {1: 0, 2: 3}[g]) if g in (1, 2) else None


def split_kernel(rows, slot_width, scalars, source, *outputs):
    tiles = slot_width // LANES
    group, position = scalars[2 * IRREPS], scalars[2 * IRREPS + 1]
    lane = lax.broadcasted_iota(jnp.int32, (rows, LANES), 1)
    for slot in range(IRREPS):
        irrep = jnp.int32(0)
        for h in range(IRREPS):
            irrep = jnp.where(scalars[h] == (group ^ slot), h, irrep)
        size = scalars[IRREPS + irrep]
        high, low = outputs[2 * slot], outputs[2 * slot + 1]
        for tile in range(tiles):
            first = position * slot_width + tile * LANES
            limit = jnp.where(first // BLOCK < size, size - first % BLOCK, 0)
            value = source[pl.ds(tile * IRREPS + irrep, rows, stride=tiles * IRREPS), :]
            value = jnp.where(lane < limit, value, 0.0)
            rounded = value.astype(jnp.bfloat16)
            place = slice(tile * LANES, (tile + 1) * LANES)
            if slot == IRREPS - 1 and tile >= tiles // 2:
                outputs[-1][:, (tile - tiles // 2) * LANES : (tile + 1 - tiles // 2) * LANES] = value
            high[:, place] = rounded
            low[:, place] = (value - rounded.astype(jnp.float32)).astype(jnp.bfloat16)


def split_rows(amplitudes, scalars):
    pairs, _, slot_width = amplitudes.shape
    rows = 64
    view = amplitudes.reshape(pairs, IRREPS, slot_width // LANES, LANES).transpose(0, 2, 1, 3).reshape(-1, LANES)
    return pl.pallas_call(
        functools.partial(split_kernel, rows, slot_width),
        out_shape=[pltpu.HBM((pairs, slot_width), jnp.bfloat16)] * (2 * IRREPS)
        + [pltpu.HBM((pairs, slot_width // 2), jnp.float32)],
        grid_spec=pltpu.PrefetchScalarGridSpec(
            num_scalar_prefetch=1,
            grid=(pairs // rows,),
            in_specs=[pl.BlockSpec((rows * IRREPS * slot_width // LANES, LANES), lambda i, scalars: (i, 0))],
            out_specs=[pl.BlockSpec((rows, slot_width), lambda i, scalars: (i, 0))] * (2 * IRREPS)
            + [pl.BlockSpec((rows, slot_width // 2), lambda i, scalars: (i, 0))],
        ),
        compiler_params=pltpu.CompilerParams(vmem_limit_bytes=16 << 20),
        cost_estimate=pl.CostEstimate(flops=0, bytes_accessed=8 * pairs * IRREPS * slot_width, transcendentals=0),
        name="split_rows",
    )(scalars, *in_hbm([view]))


PARTS = 2


def halves_of(value):
    rounded = value.astype(jnp.bfloat16)
    return rounded, (value - rounded.astype(jnp.float32)).astype(jnp.bfloat16)


def split_dot(left, right):
    dot = functools.partial(jnp.dot, preferred_element_type=jnp.float32)
    return dot(left[0], right[0]) + (dot(left[0], right[1]) + dot(left[1], right[0]))


def in_hbm(values):
    return [pltpu.with_memory_space_constraint(value, pltpu.HBM) for value in values]


def product_kernel(kind, scalars, *refs):
    slabs, (high, low, out, high_here, low_here, slab_here, total, sems) = refs[:-8], refs[-8:]
    depth = high.shape[1] // PARTS
    places = [pl.ds(part * depth, depth) for part in range(PARTS)]
    group = scalars[2 * IRREPS]
    ends = (group == 0) | (group == NG - 1)
    inner = jnp.logical_not(ends)

    def copies_of(part, slab):
        place = places[part]
        return [
            pltpu.make_async_copy(slab.at[place, :], slab_here.at[place, :], sems.at[part, 0]),
            pltpu.make_async_copy(high.at[:, place], high_here.at[:, place], sems.at[part, 1]),
            pltpu.make_async_copy(low.at[:, place], low_here.at[:, place], sems.at[part, 2]),
        ]

    def start(part, slab):
        for copy in copies_of(part, slab):
            copy.start()

    def add(part, first):
        for copy in copies_of(part, slabs[-1]):
            copy.wait()
        right = halves_of(slab_here[places[part], :])
        term = split_dot((high_here[:, places[part]], low_here[:, places[part]]), right)
        total[...] = term if first else total[...] + term

    if kind == "one":
        start(0, slabs[0])
        start(1, slabs[0])
    else:

        @pl.when(ends)
        def _():
            start(0, slabs[0])
            if kind == "two":
                start(1, slabs[0])

        @pl.when(inner)
        def _():
            start(0, slabs[1])
            start(1, slabs[1])

    add(0, True)
    if kind == "last":
        pl.when(inner)(lambda: add(1, False))
    else:
        add(1, False)
    out[...] = total[...].T


def product(kind, scalars, slabs, high, low):
    columns = slabs[0].shape[1]
    pairs, slots = high.shape
    return pl.pallas_call(
        functools.partial(product_kernel, kind),
        out_shape=jax.ShapeDtypeStruct((columns, pairs), jnp.float32),
        in_specs=[pl.BlockSpec(memory_space=pltpu.SMEM)] + [pl.BlockSpec(memory_space=pl.ANY)] * (len(slabs) + 2),
        out_specs=pl.BlockSpec(memory_space=pltpu.VMEM),
        scratch_shapes=[pltpu.VMEM((pairs, slots), jnp.bfloat16)] * 2
        + [
            pltpu.VMEM((slots, columns), jnp.float32),
            pltpu.VMEM((pairs, columns), jnp.float32),
            pltpu.SemaphoreType.DMA((PARTS, 3)),
        ],
        compiler_params=pltpu.CompilerParams(vmem_limit_bytes=12 << 20),
        cost_estimate=pl.CostEstimate(
            flops=6 * slots * columns * pairs, bytes_accessed=4 * slots * (columns + pairs), transcendentals=0
        ),
        name="product",
    )(scalars, *in_hbm([*slabs, high, low]))


def guest_kernel(slab, rows, out, slab_here, rows_here, sems):
    depth = rows.shape[1]
    copies = [
        pltpu.make_async_copy(slab.at[pl.ds(depth, depth), :], slab_here, sems.at[0]),
        pltpu.make_async_copy(rows, rows_here, sems.at[1]),
    ]
    for copy in copies:
        copy.start()
    for copy in copies:
        copy.wait()
    out[...] = split_dot(halves_of(rows_here[...]), halves_of(slab_here[...])).T


def guest_product(slab, rows):
    columns = slab.shape[1]
    pairs, depth = rows.shape
    return pl.pallas_call(
        guest_kernel,
        out_shape=jax.ShapeDtypeStruct((columns, pairs), jnp.float32),
        in_specs=[pl.BlockSpec(memory_space=pl.ANY)] * 2,
        out_specs=pl.BlockSpec(memory_space=pltpu.VMEM),
        scratch_shapes=[
            pltpu.VMEM((depth, columns), jnp.float32),
            pltpu.VMEM((pairs, depth), jnp.float32),
            pltpu.SemaphoreType.DMA((2,)),
        ],
        compiler_params=pltpu.CompilerParams(vmem_limit_bytes=12 << 20),
        cost_estimate=pl.CostEstimate(
            flops=6 * depth * columns * pairs, bytes_accessed=4 * depth * (columns + pairs), transcendentals=0
        ),
        name="guest_product",
    )(*in_hbm([slab, rows]))


def finish_kernel(column_width, scalars, *refs):
    parts, out = refs[:-1], refs[-1]
    group, position = scalars[2 * IRREPS], scalars[2 * IRREPS + 1]
    column = position * column_width + lax.broadcasted_iota(jnp.int32, out.shape[1:], 0)
    for irrep in range(IRREPS):
        slot = scalars[irrep] ^ group
        size = scalars[IRREPS + irrep]
        total = parts[0][slot]
        for part in parts[1:]:
            total = total + part[slot]
        valid = (column // BLOCK < size) & (column % BLOCK < size)
        out[irrep] = jnp.where(valid, total, 0.0)


def finish(scalars, parts):
    vmem = pl.BlockSpec(memory_space=pltpu.VMEM)
    return pl.pallas_call(
        functools.partial(finish_kernel, parts[0].shape[1]),
        out_shape=jax.ShapeDtypeStruct(parts[0].shape, jnp.float32),
        in_specs=[pl.BlockSpec(memory_space=pltpu.SMEM)] + [vmem] * len(parts),
        out_specs=vmem,
        compiler_params=pltpu.CompilerParams(vmem_limit_bytes=4 << 20),
        name="finish",
    )(scalars, *parts)


def local(amplitudes, integrals, irrep_sizes, owner_map):
    pairs = amplitudes.shape[0]
    rows, columns = integrals.shape[1:]
    column_width = columns // lax.axis_size("blk")
    position = lax.axis_index("blk")
    group = lax.axis_index("grp")
    core = position % NC
    z_part = (position // NC) % NZ

    own = integrals[0]
    near = permute(own, pair_swap)
    middle = permute(own, middle_swap)
    scalars = jnp.concatenate([owner_map, irrep_sizes, jnp.stack([group, position])])
    *split, moved = split_rows(amplitudes, scalars)
    guests = permute(moved, inward)
    crossed = permute(near, middle_swap)
    passed = permute(middle, outward)
    far = permute(crossed[: rows // 2], outward)

    def by_plane(result):
        return result.reshape(NY * NX, columns // (NY * NX), pairs)

    def columns_of(kind, slot, *slabs):
        return by_plane(product(kind, scalars, slabs, split[2 * slot], split[2 * slot + 1]))

    first = plane_sum(jnp.concatenate([columns_of("one", 0, own), columns_of("one", 1, near)], axis=1))
    guest = by_plane(guest_product(crossed, guests))
    second = plane_sum(jnp.concatenate([columns_of("two", 2, passed, crossed), guest], axis=1))
    second, handed = jnp.split(second, 2)
    third = plane_sum(columns_of("last", 3, far, middle))
    third = third + permute(handed, outward)
    total = jnp.concatenate([first, second, third], axis=0).reshape(IRREPS, NZ * NC, column_width, pairs)

    def share(flip):
        here = (z_part * NC + core) ^ flip
        return lax.dynamic_index_in_dim(total, here, 1, keepdims=False)

    parts = [share(0)]
    for flip in (3, 2, 1):
        parts.append(permute(share(flip), lambda y, x, z, c, g: (y, x, z ^ (flip >> 1), c ^ (flip & 1), g)))
    return jnp.transpose(finish(scalars, parts), (2, 0, 1))


def solution(mesh):
    in_specs = (P("grp", None, "blk"), P("grp", "blk", None), P(), P())
    out_specs = P("grp", None, "blk")
    return jax.shard_map(local, mesh=mesh, in_specs=in_specs, out_specs=out_specs, check_vma=False)
```

```python
import functools

import jax
import jax.numpy as jnp
from jax import lax
from jax.experimental import pallas as pl
from jax.experimental.pallas import tpu as pltpu
from jax.sharding import PartitionSpec as P


BLOCK = 256
IRREPS = 4
LANES = 128
NY, NX, NZ, NC, NG = 4, 4, 2, 2, 4
AXES = ("blk", "grp")


def blk_index(y, x, z, c):
    return ((y * NX + x) * NZ + z) * NC + c


def every_device():
    for y in range(NY):
        for x in range(NX):
            for z in range(NZ):
                for c in range(NC):
                    for g in range(NG):
                        yield y, x, z, c, g


def permute(value, target):
    pairs = []
    for place in every_device():
        there = target(*place)
        if there is None:
            continue
        pairs.append((blk_index(*place[:4]) * NG + place[4], blk_index(*there[:4]) * NG + there[4]))
    return lax.ppermute(value, AXES, pairs)


def plane_groups():
    return [[blk_index(y, x, z, c) for y in range(NY) for x in range(NX)] for z in range(NZ) for c in range(NC)]


def plane_sum(chip):
    spread = lax.all_to_all(chip, "blk", 0, 0, tiled=True, axis_index_groups=plane_groups())
    return jnp.sum(spread, axis=0)


def pair_swap(y, x, z, c, g):
    return y, x, z, c, g ^ 1


def middle_swap(y, x, z, c, g):
    return (y, x, z, c, 3 - g) if g in (1, 2) else None


def inward(y, x, z, c, g):
    return (y, x, z, c, {0: 1, 3: 2}[g]) if g in (0, 3) else None


def outward(y, x, z, c, g):
    return (y, x, z, c, {1: 0, 2: 3}[g]) if g in (1, 2) else None


def split_kernel(rows, slot_width, scalars, source, *outputs):
    tiles = slot_width // LANES
    group, position = scalars[2 * IRREPS], scalars[2 * IRREPS + 1]
    lane = lax.broadcasted_iota(jnp.int32, (rows, LANES), 1)
    for slot in range(IRREPS):
        irrep = jnp.int32(0)
        for h in range(IRREPS):
            irrep = jnp.where(scalars[h] == (group ^ slot), h, irrep)
        size = scalars[IRREPS + irrep]
        high, low = outputs[2 * slot], outputs[2 * slot + 1]
        for tile in range(tiles):
            first = position * slot_width + tile * LANES
            limit = jnp.where(first // BLOCK < size, size - first % BLOCK, 0)
            value = source[pl.ds(tile * IRREPS + irrep, rows, stride=tiles * IRREPS), :]
            value = jnp.where(lane < limit, value, 0.0)
            rounded = value.astype(jnp.bfloat16)
            place = slice(tile * LANES, (tile + 1) * LANES)
            if slot == IRREPS - 1 and tile >= tiles // 2:
                outputs[-1][:, (tile - tiles // 2) * LANES : (tile + 1 - tiles // 2) * LANES] = value
            high[:, place] = rounded
            low[:, place] = (value - rounded.astype(jnp.float32)).astype(jnp.bfloat16)


def split_rows(amplitudes, scalars):
    pairs, _, slot_width = amplitudes.shape
    rows = 64
    view = amplitudes.reshape(pairs, IRREPS, slot_width // LANES, LANES).transpose(0, 2, 1, 3).reshape(-1, LANES)
    return pl.pallas_call(
        functools.partial(split_kernel, rows, slot_width),
        out_shape=[pltpu.HBM((pairs, slot_width), jnp.bfloat16)] * (2 * IRREPS)
        + [pltpu.HBM((pairs, slot_width // 2), jnp.float32)],
        grid_spec=pltpu.PrefetchScalarGridSpec(
            num_scalar_prefetch=1,
            grid=(pairs // rows,),
            in_specs=[pl.BlockSpec((rows * IRREPS * slot_width // LANES, LANES), lambda i, scalars: (i, 0))],
            out_specs=[pl.BlockSpec((rows, slot_width), lambda i, scalars: (i, 0))] * (2 * IRREPS)
            + [pl.BlockSpec((rows, slot_width // 2), lambda i, scalars: (i, 0))],
        ),
        compiler_params=pltpu.CompilerParams(vmem_limit_bytes=16 << 20),
        cost_estimate=pl.CostEstimate(flops=0, bytes_accessed=8 * pairs * IRREPS * slot_width, transcendentals=0),
        name="split_rows",
    )(scalars, *in_hbm([view]))


PARTS = 4


def halves_of(value):
    rounded = value.astype(jnp.bfloat16)
    return rounded, (value - rounded.astype(jnp.float32)).astype(jnp.bfloat16)


def split_dot(left, right):
    dot = functools.partial(jnp.dot, preferred_element_type=jnp.float32)
    return dot(left[0], right[0]) + (dot(left[0], right[1]) + dot(left[1], right[0]))


def in_hbm(values):
    return [pltpu.with_memory_space_constraint(value, pltpu.HBM) for value in values]


def part_copies(part, sources, here, sems):
    slab, high, low = sources
    slab_here, high_here, low_here = here
    depth = high.shape[1] // PARTS
    place = pl.ds(part * depth, depth)
    return [
        pltpu.make_async_copy(slab.at[place, :], slab_here.at[place, :], sems.at[part, 0]),
        pltpu.make_async_copy(high.at[:, place], high_here.at[:, place], sems.at[part, 1]),
        pltpu.make_async_copy(low.at[:, place], low_here.at[:, place], sems.at[part, 2]),
    ]


def start_parts(parts, sources, here, sems):
    for part in parts:
        for copy in part_copies(part, sources, here, sems):
            copy.start()


def add_parts(parts, sources, here, sems, total):
    slab_here, high_here, low_here = here
    depth = high_here.shape[1] // PARTS
    for part in parts:
        for copy in part_copies(part, sources, here, sems):
            copy.wait()
        place = pl.ds(part * depth, depth)
        term = split_dot((high_here[:, place], low_here[:, place]), halves_of(slab_here[place, :]))
        total[...] = term if part == 0 else total[...] + term


def is_end(scalars):
    group = scalars[2 * IRREPS]
    return (group == 0) | (group == NG - 1)


def put_halves(scalars, total, kept, sent, index):
    groups, width, half = kept.shape[0], kept.shape[1] // 2, kept.shape[2]
    core = scalars[2 * IRREPS + 1] % NC
    for out, which in ((sent, 1 - core), (kept, core)):
        rows = total[pl.ds(pl.multiple_of(which * half, half), half), :]
        out[:, index * width : (index + 1) * width, :] = rows.T.reshape(groups, width, half)


def first_kernel(scalars, own, near, high_0, low_0, high_1, low_1, kept, sent, slabs, highs, lows, total, sems):
    sources = ((own, high_0, low_0), (near, high_1, low_1))
    here = [(slabs.at[k], highs.at[k], lows.at[k]) for k in range(2)]
    for k in range(2):
        start_parts(range(PARTS), sources[k], here[k], sems.at[k])
    for k in range(2):
        add_parts(range(PARTS), sources[k], here[k], sems.at[k], total)
        put_halves(scalars, total, kept, sent, k)


def second_kernel(
    scalars, passed, crossed, guests, high, low, kept, sent, slab, high_here, low_here, guest_slab, rows, total, sems, guest_sems
):
    depth = rows.shape[1]
    here = (slab, high_here, low_here)
    ends = is_end(scalars)
    pl.when(ends)(lambda: start_parts(range(PARTS), (passed, high, low), here, sems))
    pl.when(jnp.logical_not(ends))(lambda: start_parts(range(PARTS), (crossed, high, low), here, sems))
    guest_copies = [
        pltpu.make_async_copy(crossed.at[pl.ds(depth, depth), :], guest_slab, guest_sems.at[0]),
        pltpu.make_async_copy(guests, rows, guest_sems.at[1]),
    ]
    for copy in guest_copies:
        copy.start()
    add_parts(range(PARTS), (crossed, high, low), here, sems, total)
    put_halves(scalars, total, kept, sent, 0)
    for copy in guest_copies:
        copy.wait()
    total[...] = split_dot(halves_of(rows[...]), halves_of(guest_slab[...]))
    put_halves(scalars, total, kept, sent, 1)


def last_kernel(scalars, far, middle, high, low, out, slab, high_here, low_here, total, sems):
    here = (slab, high_here, low_here)
    ends = is_end(scalars)
    inner = jnp.logical_not(ends)
    front, back = range(PARTS // 2), range(PARTS // 2, PARTS)
    pl.when(ends)(lambda: start_parts(front, (far, high, low), here, sems))
    pl.when(inner)(lambda: start_parts(range(PARTS), (middle, high, low), here, sems))
    add_parts(front, (middle, high, low), here, sems, total)
    pl.when(inner)(lambda: add_parts(back, (middle, high, low), here, sems, total))
    out[...] = total[...].T.reshape(out.shape)


def call_product(kernel, scalars, slabs, split, out_shapes, scratch, terms):
    count = len(out_shapes)
    vmem = pl.BlockSpec(memory_space=pltpu.VMEM)
    return pl.pallas_call(
        kernel,
        out_shape=[jax.ShapeDtypeStruct(shape, jnp.float32) for shape in out_shapes],
        in_specs=[pl.BlockSpec(memory_space=pltpu.SMEM)] + [pl.BlockSpec(memory_space=pl.ANY)] * (len(slabs) + len(split)),
        out_specs=[vmem] * count,
        scratch_shapes=scratch,
        compiler_params=pltpu.CompilerParams(vmem_limit_bytes=16 << 20),
        cost_estimate=pl.CostEstimate(flops=6 * terms, bytes_accessed=6 << 20, transcendentals=0),
    )(scalars, *slabs, *in_hbm(split))


def finish_kernel(column_width, scalars, *refs):
    parts, out = refs[:-1], refs[-1]
    half = parts[0].shape[2]
    group, position = scalars[2 * IRREPS], scalars[2 * IRREPS + 1]
    core = position % NC
    column = position * column_width + lax.broadcasted_iota(jnp.int32, parts[0].shape[1:], 0)
    for irrep in range(IRREPS):
        slot = scalars[irrep] ^ group
        size = scalars[IRREPS + irrep]
        valid = (column // BLOCK < size) & (column % BLOCK < size)
        mine = parts[0][slot] + parts[2][slot]
        other = parts[1][slot] + parts[3][slot]
        for k in range(NC):
            both = (parts[0][IRREPS + k] + parts[2][IRREPS + k]) + (parts[1][IRREPS + k] + parts[3][IRREPS + k])
            value = jnp.where(core == k, mine, other) + jnp.where(slot == IRREPS - 1, both, 0.0)
            out[irrep, :, k * half : (k + 1) * half] = jnp.where(valid, value, 0.0)


def finish(scalars, parts):
    _, column_width, half = parts[0].shape
    vmem = pl.BlockSpec(memory_space=pltpu.VMEM)
    return pl.pallas_call(
        functools.partial(finish_kernel, column_width),
        out_shape=jax.ShapeDtypeStruct((IRREPS, column_width, NC * half), jnp.float32),
        in_specs=[pl.BlockSpec(memory_space=pltpu.SMEM)] + [vmem] * len(parts),
        out_specs=vmem,
        compiler_params=pltpu.CompilerParams(vmem_limit_bytes=4 << 20),
        name="finish",
    )(scalars, *parts)


def local(amplitudes, integrals, irrep_sizes, owner_map):
    pairs, _, slots = amplitudes.shape
    rows, columns = integrals.shape[1:]
    column_width = columns // lax.axis_size("blk")
    plane = NY * NX
    width = columns // plane
    half = pairs // NC
    position = lax.axis_index("blk")
    group = lax.axis_index("grp")
    core = position % NC
    z_part = (position // NC) % NZ

    own = integrals[0]
    near = permute(own, pair_swap)
    middle = permute(own, middle_swap)
    scalars = jnp.concatenate([owner_map, irrep_sizes, jnp.stack([group, position])])
    *split, moved = split_rows(amplitudes, scalars)
    guests = permute(moved, inward)
    crossed = permute(near, middle_swap)
    passed = permute(middle, outward)
    far = permute(crossed[: rows // 2], outward)

    matrix = pltpu.VMEM((pairs, slots), jnp.bfloat16)
    slab = pltpu.VMEM((rows, columns), jnp.float32)
    total = pltpu.VMEM((pairs, columns), jnp.float32)
    sems = pltpu.SemaphoreType.DMA((PARTS, 3))
    terms = pairs * columns * slots
    joint = [(plane, 2 * width, half)] * 2

    def chip_sum(kept, sent):
        return kept + permute(sent, lambda y, x, z, c, g: (y, x, z, 1 - c, g))

    scratch = [
        pltpu.VMEM((2, rows, columns), jnp.float32),
        pltpu.VMEM((2, pairs, slots), jnp.bfloat16),
        pltpu.VMEM((2, pairs, slots), jnp.bfloat16),
        total,
        pltpu.SemaphoreType.DMA((2, PARTS, 3)),
    ]
    result = call_product(first_kernel, scalars, [own, near], split[:4], joint, scratch, 2 * terms)
    first_chip = chip_sum(*result)
    first = plane_sum(first_chip)
    scratch = [
        slab,
        matrix,
        matrix,
        pltpu.VMEM((rows // 2, columns), jnp.float32),
        pltpu.VMEM((pairs, slots // 2), jnp.float32),
        total,
        sems,
        pltpu.SemaphoreType.DMA((2,)),
    ]
    result = call_product(second_kernel, scalars, [passed, crossed, guests], split[4:6], joint, scratch, 2 * terms)
    second_chip = chip_sum(*result)
    second = plane_sum(second_chip)
    scratch = [slab, matrix, matrix, total, sems]
    (result,) = call_product(last_kernel, scalars, [far, middle], split[6:], [(plane, width, pairs)], scratch, terms)
    third = plane_sum(result)
    third = third.reshape(width, NC, half).swapaxes(0, 1)
    handed = permute(second[width:], outward)
    units = jnp.concatenate([first.reshape(2, width, half), second[None, :width], handed[None], third], axis=0)
    units = units.reshape(-1, NZ * NC, column_width, half)

    def share(flip):
        here = (z_part * NC + core) ^ flip
        return lax.dynamic_index_in_dim(units, here, 1, keepdims=False)

    parts = [share(0)] + [None] * 3
    for flip in (3, 2, 1):
        parts[flip] = permute(share(flip), lambda y, x, z, c, g: (y, x, z ^ (flip >> 1), c ^ (flip & 1), g))
    return jnp.transpose(finish(scalars, parts), (2, 0, 1))


def solution(mesh):
    in_specs = (P("grp", None, "blk"), P("grp", "blk", None), P(), P())
    out_specs = P("grp", None, "blk")
    return jax.shard_map(local, mesh=mesh, in_specs=in_specs, out_specs=out_specs, check_vma=False)
```

```python
import functools

import jax
import jax.numpy as jnp
from jax import lax
from jax.experimental import pallas as pl
from jax.experimental.pallas import tpu as pltpu
from jax.sharding import PartitionSpec as P


BLOCK = 256
IRREPS = 4
LANES = 128
NY, NX, NZ, NC, NG = 4, 4, 2, 2, 4
AXES = ("blk", "grp")


def blk_index(y, x, z, c):
    return ((y * NX + x) * NZ + z) * NC + c


def every_device():
    for y in range(NY):
        for x in range(NX):
            for z in range(NZ):
                for c in range(NC):
                    for g in range(NG):
                        yield y, x, z, c, g


def permute(value, target):
    pairs = []
    for place in every_device():
        there = target(*place)
        if there is None:
            continue
        pairs.append((blk_index(*place[:4]) * NG + place[4], blk_index(*there[:4]) * NG + there[4]))
    return lax.ppermute(value, AXES, pairs)


def plane_groups():
    return [[blk_index(y, x, z, c) for y in range(NY) for x in range(NX)] for z in range(NZ) for c in range(NC)]


def plane_sum(chip):
    spread = lax.all_to_all(chip, "blk", 0, 0, tiled=True, axis_index_groups=plane_groups())
    return jnp.sum(spread, axis=0)


def staged_sum(chip, position):
    y, x = position // (NX * NZ * NC), (position // (NZ * NC)) % NX

    def stage(value, place, count, target):
        def block(step):
            return lax.dynamic_index_in_dim(value, (place + step) % count, 0, keepdims=False)

        arrived = [permute(block(step), functools.partial(target, step)) for step in (2, 1, 3)]
        return block(0) + ((arrived[1] + arrived[2]) + arrived[0])

    rows = stage(chip.reshape(NY, NX, *chip.shape[1:]), y, NY, lambda k, y, x, z, c, g: ((y + k) % NY, x, z, c, g))
    return stage(rows, x, NX, lambda k, y, x, z, c, g: (y, (x + k) % NX, z, c, g))


def pair_swap(y, x, z, c, g):
    return y, x, z, c, g ^ 1


def middle_swap(y, x, z, c, g):
    return (y, x, z, c, 3 - g) if g in (1, 2) else None


def inward(y, x, z, c, g):
    return (y, x, z, c, {0: 1, 3: 2}[g]) if g in (0, 3) else None


def outward(y, x, z, c, g):
    return (y, x, z, c, {1: 0, 2: 3}[g]) if g in (1, 2) else None


def split_kernel(rows, slot_width, scalars, source, *outputs):
    tiles = slot_width // LANES
    group, position = scalars[2 * IRREPS], scalars[2 * IRREPS + 1]
    lane = lax.broadcasted_iota(jnp.int32, (rows, LANES), 1)
    for slot in range(IRREPS):
        irrep = jnp.int32(0)
        for h in range(IRREPS):
            irrep = jnp.where(scalars[h] == (group ^ slot), h, irrep)
        size = scalars[IRREPS + irrep]
        high, low = outputs[2 * slot], outputs[2 * slot + 1]
        for tile in range(tiles):
            first = position * slot_width + tile * LANES
            limit = jnp.where(first // BLOCK < size, size - first % BLOCK, 0)
            value = source[pl.ds(tile * IRREPS + irrep, rows, stride=tiles * IRREPS), :]
            value = jnp.where(lane < limit, value, 0.0)
            rounded = value.astype(jnp.bfloat16)
            place = slice(tile * LANES, (tile + 1) * LANES)
            if slot == IRREPS - 1 and tile >= tiles // 2:
                outputs[-1][:, (tile - tiles // 2) * LANES : (tile + 1 - tiles // 2) * LANES] = value
            high[:, place] = rounded
            low[:, place] = (value - rounded.astype(jnp.float32)).astype(jnp.bfloat16)


def split_rows(amplitudes, scalars):
    pairs, _, slot_width = amplitudes.shape
    rows = 64
    view = amplitudes.reshape(pairs, IRREPS, slot_width // LANES, LANES).transpose(0, 2, 1, 3).reshape(-1, LANES)
    return pl.pallas_call(
        functools.partial(split_kernel, rows, slot_width),
        out_shape=[pltpu.HBM((pairs, slot_width), jnp.bfloat16)] * (2 * IRREPS)
        + [pltpu.HBM((pairs, slot_width // 2), jnp.float32)],
        grid_spec=pltpu.PrefetchScalarGridSpec(
            num_scalar_prefetch=1,
            grid=(pairs // rows,),
            in_specs=[pl.BlockSpec((rows * IRREPS * slot_width // LANES, LANES), lambda i, scalars: (i, 0))],
            out_specs=[pl.BlockSpec((rows, slot_width), lambda i, scalars: (i, 0))] * (2 * IRREPS)
            + [pl.BlockSpec((rows, slot_width // 2), lambda i, scalars: (i, 0))],
        ),
        compiler_params=pltpu.CompilerParams(vmem_limit_bytes=16 << 20),
        cost_estimate=pl.CostEstimate(flops=0, bytes_accessed=8 * pairs * IRREPS * slot_width, transcendentals=0),
        name="split_rows",
    )(scalars, *in_hbm([view]))


PARTS = 4


def halves_of(value):
    rounded = value.astype(jnp.bfloat16)
    return rounded, (value - rounded.astype(jnp.float32)).astype(jnp.bfloat16)


def split_dot(left, right):
    dot = functools.partial(jnp.dot, preferred_element_type=jnp.float32)
    return dot(left[0], right[0]) + (dot(left[0], right[1]) + dot(left[1], right[0]))


def in_hbm(values):
    return [pltpu.with_memory_space_constraint(value, pltpu.HBM) for value in values]


def part_copies(part, sources, here, sems):
    slabs, high, low = sources
    slab_here, high_here, low_here = here
    depth = high.shape[1] // PARTS
    place = pl.ds(part * depth, depth)
    pieces, first = slabs[0].shape[0] // depth, part * depth
    slab = slabs[min(part // pieces, len(slabs) - 1)]
    there = pl.ds(first % slabs[0].shape[0], depth)
    return [
        pltpu.make_async_copy(slab.at[there, :], slab_here.at[place, :], sems.at[part, 0]),
        pltpu.make_async_copy(high.at[:, place], high_here.at[:, place], sems.at[part, 1]),
        pltpu.make_async_copy(low.at[:, place], low_here.at[:, place], sems.at[part, 2]),
    ]


def start_parts(parts, sources, here, sems):
    for part in parts:
        for copy in part_copies(part, sources, here, sems):
            copy.start()


def add_parts(parts, sources, here, sems, total):
    slab_here, high_here, low_here = here
    depth = high_here.shape[1] // PARTS
    for part in parts:
        for copy in part_copies(part, sources, here, sems):
            copy.wait()
        place = pl.ds(part * depth, depth)
        term = split_dot((high_here[:, place], low_here[:, place]), halves_of(slab_here[place, :]))
        total[...] = term if part == 0 else total[...] + term


def is_end(scalars):
    group = scalars[2 * IRREPS]
    return (group == 0) | (group == NG - 1)


def put_halves(scalars, total, kept, sent, index):
    groups, width, half = kept.shape[0], kept.shape[1] // 2, kept.shape[2]
    core = scalars[2 * IRREPS + 1] % NC
    for out, which in ((sent, 1 - core), (kept, core)):
        rows = total[pl.ds(pl.multiple_of(which * half, half), half), :]
        out[:, index * width : (index + 1) * width, :] = rows.T.reshape(groups, width, half)


def first_kernel(scalars, own, near_a, near_b, high_0, low_0, high_1, low_1, kept, sent, slabs, highs, lows, total, sems):
    sources = (((own,), high_0, low_0), ((near_a, near_b), high_1, low_1))
    here = [(slabs.at[k], highs.at[k], lows.at[k]) for k in range(2)]
    for k in range(2):
        start_parts(range(PARTS), sources[k], here[k], sems.at[k])
    for k in range(2):
        add_parts(range(PARTS), sources[k], here[k], sems.at[k], total)
        put_halves(scalars, total, kept, sent, k)


def guest_kernel(slab, rows, out, slab_here, rows_here, sems):
    copies = [
        pltpu.make_async_copy(slab, slab_here, sems.at[0]),
        pltpu.make_async_copy(rows, rows_here, sems.at[1]),
    ]
    for copy in copies:
        copy.start()
    for copy in copies:
        copy.wait()
    out[...] = split_dot(halves_of(rows_here[...]), halves_of(slab_here[...]))


def second_kernel(
    scalars, passed_a, passed_b, crossed_a, crossed_b, guest, high, low, kept, sent, slab, high_here, low_here, total, sems, guest_sem
):
    here = (slab, high_here, low_here)
    ends = is_end(scalars)
    crossed = ((crossed_a, crossed_b), high, low)
    pl.when(ends)(lambda: start_parts(range(PARTS), ((passed_a, passed_b), high, low), here, sems))
    pl.when(jnp.logical_not(ends))(lambda: start_parts(range(PARTS), crossed, here, sems))
    guest_copy = pltpu.make_async_copy(guest, total.at[1], guest_sem)
    guest_copy.start()
    add_parts(range(PARTS), crossed, here, sems, total.at[0])
    put_halves(scalars, total.at[0], kept, sent, 0)
    guest_copy.wait()
    put_halves(scalars, total.at[1], kept, sent, 1)


def last_kernel(scalars, far, middle_a, middle_b, high, low, out, slab, high_here, low_here, total, sems):
    here = (slab, high_here, low_here)
    ends = is_end(scalars)
    inner = jnp.logical_not(ends)
    front, back = range(PARTS // 2), range(PARTS // 2, PARTS)
    middle = ((middle_a, middle_b), high, low)
    pl.when(ends)(lambda: start_parts(front, ((far,), high, low), here, sems))
    pl.when(inner)(lambda: start_parts(range(PARTS), middle, here, sems))
    add_parts(front, middle, here, sems, total)
    pl.when(inner)(lambda: add_parts(back, middle, here, sems, total))
    out[...] = total[...].T.reshape(out.shape)


def guest_product(slab, rows):
    pairs, columns = rows.shape[0], slab.shape[1]
    return pl.pallas_call(
        guest_kernel,
        out_shape=jax.ShapeDtypeStruct((pairs, columns), jnp.float32),
        in_specs=[pl.BlockSpec(memory_space=pl.ANY)] * 2,
        out_specs=pl.BlockSpec(memory_space=pltpu.VMEM),
        scratch_shapes=[
            pltpu.VMEM(slab.shape, jnp.float32),
            pltpu.VMEM(rows.shape, jnp.float32),
            pltpu.SemaphoreType.DMA((2,)),
        ],
        compiler_params=pltpu.CompilerParams(vmem_limit_bytes=12 << 20),
        cost_estimate=pl.CostEstimate(flops=6 * pairs * rows.shape[1] * columns, bytes_accessed=2 << 20, transcendentals=0),
        name="guest_product",
    )(slab, rows)


def call_product(kernel, scalars, slabs, split, out_shapes, scratch, terms):
    count = len(out_shapes)
    vmem = pl.BlockSpec(memory_space=pltpu.VMEM)
    return pl.pallas_call(
        kernel,
        out_shape=[jax.ShapeDtypeStruct(shape, jnp.float32) for shape in out_shapes],
        in_specs=[pl.BlockSpec(memory_space=pltpu.SMEM)] + [pl.BlockSpec(memory_space=pl.ANY)] * (len(slabs) + len(split)),
        out_specs=[vmem] * count,
        scratch_shapes=scratch,
        compiler_params=pltpu.CompilerParams(vmem_limit_bytes=16 << 20),
        cost_estimate=pl.CostEstimate(flops=6 * terms, bytes_accessed=6 << 20, transcendentals=0),
    )(scalars, *slabs, *in_hbm(split))


def finish_kernel(column_width, scalars, *refs):
    parts, out = refs[:-1], refs[-1]
    half = parts[0].shape[2]
    group, position = scalars[2 * IRREPS], scalars[2 * IRREPS + 1]
    core = position % NC
    column = position * column_width + lax.broadcasted_iota(jnp.int32, parts[0].shape[1:], 0)
    for irrep in range(IRREPS):
        slot = scalars[irrep] ^ group
        size = scalars[IRREPS + irrep]
        valid = (column // BLOCK < size) & (column % BLOCK < size)
        mine = parts[0][slot] + parts[2][slot]
        other = parts[1][slot] + parts[3][slot]
        for k in range(NC):
            both = (parts[0][IRREPS + k] + parts[2][IRREPS + k]) + (parts[1][IRREPS + k] + parts[3][IRREPS + k])
            value = jnp.where(core == k, mine, other) + jnp.where(slot == IRREPS - 1, both, 0.0)
            out[irrep, :, k * half : (k + 1) * half] = jnp.where(valid, value, 0.0)


def finish(scalars, parts):
    _, column_width, half = parts[0].shape
    vmem = pl.BlockSpec(memory_space=pltpu.VMEM)
    return pl.pallas_call(
        functools.partial(finish_kernel, column_width),
        out_shape=jax.ShapeDtypeStruct((IRREPS, column_width, NC * half), jnp.float32),
        in_specs=[pl.BlockSpec(memory_space=pltpu.SMEM)] + [vmem] * len(parts),
        out_specs=vmem,
        compiler_params=pltpu.CompilerParams(vmem_limit_bytes=4 << 20),
        name="finish",
    )(scalars, *parts)


def local(amplitudes, integrals, irrep_sizes, owner_map):
    pairs, _, slots = amplitudes.shape
    rows, columns = integrals.shape[1:]
    column_width = columns // lax.axis_size("blk")
    plane = NY * NX
    width = columns // plane
    half = pairs // NC
    position = lax.axis_index("blk")
    group = lax.axis_index("grp")
    core = position % NC
    z_part = (position // NC) % NZ

    own = integrals[0]
    own_a = own[: rows // 2]
    near_a = permute(own_a, pair_swap)
    middle_a = permute(own_a, middle_swap)
    own_b = lax.optimization_barrier(own)[rows // 2 :]
    near_b = permute(own_b, pair_swap)
    middle_b = permute(own_b, middle_swap)
    scalars = jnp.concatenate([owner_map, irrep_sizes, jnp.stack([group, position])])
    *split, moved = split_rows(amplitudes, scalars)
    passed_a = permute(middle_a, outward)
    crossed_a = permute(near_a, middle_swap)
    passed_b = permute(middle_b, outward)
    crossed_b = permute(near_b, middle_swap)
    guests = permute(moved, inward)
    far = permute(crossed_a, outward)

    matrix = pltpu.VMEM((pairs, slots), jnp.bfloat16)
    slab = pltpu.VMEM((rows, columns), jnp.float32)
    total = pltpu.VMEM((pairs, columns), jnp.float32)
    sems = pltpu.SemaphoreType.DMA((PARTS, 3))
    terms = pairs * columns * slots
    joint = [(plane, 2 * width, half)] * 2

    def chip_sum(kept, sent):
        return kept + permute(sent, lambda y, x, z, c, g: (y, x, z, 1 - c, g))

    scratch = [
        pltpu.VMEM((2, rows, columns), jnp.float32),
        pltpu.VMEM((2, pairs, slots), jnp.bfloat16),
        pltpu.VMEM((2, pairs, slots), jnp.bfloat16),
        total,
        pltpu.SemaphoreType.DMA((2, PARTS, 3)),
    ]
    result = call_product(first_kernel, scalars, [own, near_a, near_b], split[:4], joint, scratch, 2 * terms)
    first_chip = chip_sum(*result)
    first = plane_sum(first_chip)
    guest = guest_product(crossed_b, guests)
    scratch = [slab, matrix, matrix, pltpu.VMEM((2, pairs, columns), jnp.float32), sems, pltpu.SemaphoreType.DMA]
    slabs = [passed_a, passed_b, crossed_a, crossed_b, guest]
    result = call_product(second_kernel, scalars, slabs, split[4:6], joint, scratch, terms)
    second = staged_sum(chip_sum(*result), position)
    scratch = [slab, matrix, matrix, total, sems]
    slabs = [far, middle_a, middle_b]
    (result,) = call_product(last_kernel, scalars, slabs, split[6:], [(plane, width, pairs)], scratch, terms)
    third = staged_sum(result, position)
    third = third.reshape(width, NC, half).swapaxes(0, 1)
    handed = permute(second[width:], outward)
    units = jnp.concatenate([first.reshape(2, width, half), second[None, :width], handed[None], third], axis=0)
    units = units.reshape(-1, NZ * NC, column_width, half)

    def share(flip):
        here = (z_part * NC + core) ^ flip
        return lax.dynamic_index_in_dim(units, here, 1, keepdims=False)

    parts = [share(0)] + [None] * 3
    for flip in (3, 2, 1):
        parts[flip] = permute(share(flip), lambda y, x, z, c, g: (y, x, z ^ (flip >> 1), c ^ (flip & 1), g))
    return jnp.transpose(finish(scalars, parts), (2, 0, 1))


def solution(mesh):
    in_specs = (P("grp", None, "blk"), P("grp", "blk", None), P(), P())
    out_specs = P("grp", None, "blk")
    return jax.shard_map(local, mesh=mesh, in_specs=in_specs, out_specs=out_specs, check_vma=False)
```

```python
import functools

import jax
import jax.numpy as jnp
from jax import lax
from jax.experimental import pallas as pl
from jax.experimental.pallas import tpu as pltpu
from jax.sharding import PartitionSpec as P


BLOCK = 256
IRREPS = 4
LANES = 128
PARTS = 4
NY, NX, NZ, NC, NG = 4, 4, 2, 2, 4
AXES = ("blk", "grp")


def blk_index(y, x, z, c):
    return ((y * NX + x) * NZ + z) * NC + c


def every_device():
    for y in range(NY):
        for x in range(NX):
            for z in range(NZ):
                for c in range(NC):
                    for g in range(NG):
                        yield y, x, z, c, g


def permute(value, target):
    pairs = []
    for place in every_device():
        there = target(*place)
        if there is None:
            continue
        pairs.append((blk_index(*place[:4]) * NG + place[4], blk_index(*there[:4]) * NG + there[4]))
    return lax.ppermute(value, AXES, pairs)


def plane_groups():
    return [[blk_index(y, x, z, c) for y in range(NY) for x in range(NX)] for z in range(NZ) for c in range(NC)]


def plane_sum(chip):
    spread = lax.all_to_all(chip, "blk", 0, 0, tiled=True, axis_index_groups=plane_groups())
    return jnp.sum(spread, axis=0)


def staged_sum(chip, position):
    y, x = position // (NX * NZ * NC), (position // (NZ * NC)) % NX

    def stage(value, place, count, target):
        def block(step):
            return lax.dynamic_index_in_dim(value, (place + step) % count, 0, keepdims=False)

        arrived = [permute(block(step), functools.partial(target, step)) for step in (2, 1, 3)]
        return block(0) + ((arrived[1] + arrived[2]) + arrived[0])

    rows = stage(chip.reshape(NY, NX, *chip.shape[1:]), y, NY, lambda k, y, x, z, c, g: ((y + k) % NY, x, z, c, g))
    return stage(rows, x, NX, lambda k, y, x, z, c, g: (y, (x + k) % NX, z, c, g))


def pair_swap(y, x, z, c, g):
    return y, x, z, c, g ^ 1


def middle_swap(y, x, z, c, g):
    return (y, x, z, c, 3 - g) if g in (1, 2) else None


def inward(y, x, z, c, g):
    return (y, x, z, c, {0: 1, 3: 2}[g]) if g in (0, 3) else None


def outward(y, x, z, c, g):
    return (y, x, z, c, {1: 0, 2: 3}[g]) if g in (1, 2) else None


def split_kernel(rows, slot_width, scalars, source, *outputs):
    tiles = slot_width // LANES
    group, position = scalars[2 * IRREPS], scalars[2 * IRREPS + 1]
    lane = lax.broadcasted_iota(jnp.int32, (rows, LANES), 1)
    for slot in range(IRREPS):
        irrep = jnp.int32(0)
        for h in range(IRREPS):
            irrep = jnp.where(scalars[h] == (group ^ slot), h, irrep)
        size = scalars[IRREPS + irrep]
        high, low = outputs[2 * slot], outputs[2 * slot + 1]
        for tile in range(tiles):
            first = position * slot_width + tile * LANES
            limit = jnp.where(first // BLOCK < size, size - first % BLOCK, 0)
            value = source[pl.ds(tile * IRREPS + irrep, rows, stride=tiles * IRREPS), :]
            value = jnp.where(lane < limit, value, 0.0)
            rounded = value.astype(jnp.bfloat16)
            place = slice(tile * LANES, (tile + 1) * LANES)
            kept = tiles // PARTS
            if slot == IRREPS - 1 and tile >= kept:
                outputs[-1][:, (tile - kept) * LANES : (tile + 1 - kept) * LANES] = value
            high[:, place] = rounded
            low[:, place] = (value - rounded.astype(jnp.float32)).astype(jnp.bfloat16)


def split_rows(amplitudes, scalars):
    pairs, _, slot_width = amplitudes.shape
    rows = 64
    guest_width = slot_width - slot_width // PARTS
    view = amplitudes.reshape(pairs, IRREPS, slot_width // LANES, LANES).transpose(0, 2, 1, 3).reshape(-1, LANES)
    return pl.pallas_call(
        functools.partial(split_kernel, rows, slot_width),
        out_shape=[pltpu.HBM((pairs, slot_width), jnp.bfloat16)] * (2 * IRREPS)
        + [pltpu.HBM((pairs, guest_width), jnp.float32)],
        grid_spec=pltpu.PrefetchScalarGridSpec(
            num_scalar_prefetch=1,
            grid=(pairs // rows,),
            in_specs=[pl.BlockSpec((rows * IRREPS * slot_width // LANES, LANES), lambda i, scalars: (i, 0))],
            out_specs=[pl.BlockSpec((rows, slot_width), lambda i, scalars: (i, 0))] * (2 * IRREPS)
            + [pl.BlockSpec((rows, guest_width), lambda i, scalars: (i, 0))],
        ),
        compiler_params=pltpu.CompilerParams(vmem_limit_bytes=16 << 20),
        cost_estimate=pl.CostEstimate(flops=0, bytes_accessed=8 * pairs * IRREPS * slot_width, transcendentals=0),
        name="split_rows",
    )(scalars, *in_hbm([view]))


def halves_of(value):
    rounded = value.astype(jnp.bfloat16)
    return rounded, (value - rounded.astype(jnp.float32)).astype(jnp.bfloat16)


def split_dot(left, right):
    dot = functools.partial(jnp.dot, preferred_element_type=jnp.float32)
    return dot(left[0], right[0]) + (dot(left[0], right[1]) + dot(left[1], right[0]))


def in_hbm(values):
    return [pltpu.with_memory_space_constraint(value, pltpu.HBM) for value in values]


def part_copies(part, sources, here, sems):
    slab, high, low = sources
    slab_here, high_here, low_here = here
    depth = high.shape[1] // PARTS
    place = pl.ds(part * depth, depth)
    return [
        pltpu.make_async_copy(slab.at[place, :], slab_here.at[place, :], sems.at[part, 0]),
        pltpu.make_async_copy(high.at[:, place], high_here.at[:, place], sems.at[part, 1]),
        pltpu.make_async_copy(low.at[:, place], low_here.at[:, place], sems.at[part, 2]),
    ]


def start_parts(parts, sources, here, sems):
    for part in parts:
        for copy in part_copies(part, sources, here, sems):
            copy.start()


def add_parts(parts, sources, here, sems, total):
    slab_here, high_here, low_here = here
    depth = high_here.shape[1] // PARTS
    for part in parts:
        for copy in part_copies(part, sources, here, sems):
            copy.wait()
        place = pl.ds(part * depth, depth)
        term = split_dot((high_here[:, place], low_here[:, place]), halves_of(slab_here[place, :]))
        total[...] = term if part == 0 else total[...] + term


def is_end(scalars):
    group = scalars[2 * IRREPS]
    return (group == 0) | (group == NG - 1)


def put_halves(scalars, total, kept, sent, index):
    groups, _, half = kept.shape
    width = total.shape[1] // groups
    core = scalars[2 * IRREPS + 1] % NC
    for out, which in ((sent, 1 - core), (kept, core)):
        rows = total[pl.ds(pl.multiple_of(which * half, half), half), :]
        out[:, index * width : (index + 1) * width, :] = rows.T.reshape(groups, width, half)


def first_kernel(scalars, own, near, high_0, low_0, high_1, low_1, kept, sent, slabs, highs, lows, total, sems):
    sources = ((own, high_0, low_0), (near, high_1, low_1))
    here = [(slabs.at[k], highs.at[k], lows.at[k]) for k in range(2)]
    for k in range(2):
        start_parts(range(PARTS), sources[k], here[k], sems.at[k])
    for k in range(2):
        add_parts(range(PARTS), sources[k], here[k], sems.at[k], total)
        put_halves(scalars, total, kept, sent, k)


def guest_kernel(scalars, crossed, guests, kept, sent, slab, rows, total, sems):
    depth = rows.shape[1]
    copies = [
        pltpu.make_async_copy(crossed.at[pl.ds(crossed.shape[0] - depth, depth), :], slab, sems.at[0]),
        pltpu.make_async_copy(guests, rows, sems.at[1]),
    ]
    for copy in copies:
        copy.start()
    for copy in copies:
        copy.wait()
    total[...] = split_dot(halves_of(rows[...]), halves_of(slab[...]))
    put_halves(scalars, total, kept, sent, 0)


def second_kernel(
    scalars, passed, crossed, high, low, high_last, low_last, kept, sent, high_out, low_out, slab, high_here, low_here, total, sems, last_sems
):
    here = (slab, high_here, low_here)
    ends = is_end(scalars)
    pl.when(ends)(lambda: start_parts(range(PARTS), (passed, high, low), here, sems))
    pl.when(jnp.logical_not(ends))(lambda: start_parts(range(PARTS), (crossed, high, low), here, sems))
    copies = [
        pltpu.make_async_copy(high_last, high_out, last_sems.at[0]),
        pltpu.make_async_copy(low_last, low_out, last_sems.at[1]),
    ]
    for copy in copies:
        copy.start()
    add_parts(range(PARTS), (crossed, high, low), here, sems, total)
    put_halves(scalars, total, kept, sent, 0)
    for copy in copies:
        copy.wait()


def last_kernel(scalars, far, middle, high, low, kept, got, out, slab, total, sems):
    ends = is_end(scalars)
    inner = jnp.logical_not(ends)
    depth = far.shape[0]
    pairs = high.shape[0]

    def copy_of(source, part):
        place = pl.ds(part * depth, depth)
        return pltpu.make_async_copy(source.at[place, :], slab.at[place, :], sems.at[part])

    def add(part):
        copy_of(middle, part).wait()
        place = slice(part * depth, (part + 1) * depth)
        term = split_dot((high[:, place], low[:, place]), halves_of(slab[place, :]))
        total[...] = term if part == 0 else total[...] + term

    pl.when(ends)(lambda: copy_of(far, 0).start())

    @pl.when(inner)
    def _():
        for part in range(PARTS):
            copy_of(middle, part).start()

    out[:, :, pairs:] = kept[...] + got[...]
    add(0)

    @pl.when(inner)
    def _():
        for part in range(1, PARTS):
            add(part)

    out[:, :, :pairs] = total[...].T.reshape(out.shape[0], out.shape[1], pairs)


def call_product(kernel, scalars, moved, fixed, resident, out_shapes, scratch, terms):
    vmem = pl.BlockSpec(memory_space=pltpu.VMEM)
    return pl.pallas_call(
        kernel,
        out_shape=out_shapes,
        in_specs=[pl.BlockSpec(memory_space=pltpu.SMEM)]
        + [pl.BlockSpec(memory_space=pl.ANY)] * (len(moved) + len(fixed))
        + [vmem] * len(resident),
        out_specs=[vmem] * len(out_shapes),
        scratch_shapes=scratch,
        compiler_params=pltpu.CompilerParams(vmem_limit_bytes=16 << 20),
        cost_estimate=pl.CostEstimate(flops=6 * terms, bytes_accessed=6 << 20, transcendentals=0),
    )(scalars, *moved, *in_hbm(fixed), *resident)


def finish_kernel(column_width, scalars, *refs):
    parts, out = refs[:-1], refs[-1]
    half = parts[0].shape[2]
    group, position = scalars[2 * IRREPS], scalars[2 * IRREPS + 1]
    core = position % NC
    column = position * column_width + lax.broadcasted_iota(jnp.int32, parts[0].shape[1:], 0)
    for irrep in range(IRREPS):
        slot = scalars[irrep] ^ group
        size = scalars[IRREPS + irrep]
        valid = (column // BLOCK < size) & (column % BLOCK < size)
        mine = parts[0][slot] + parts[2][slot]
        other = parts[1][slot] + parts[3][slot]
        for k in range(NC):
            both = (parts[0][IRREPS + k] + parts[2][IRREPS + k]) + (parts[1][IRREPS + k] + parts[3][IRREPS + k])
            value = jnp.where(core == k, mine, other) + jnp.where(slot == IRREPS - 1, both, 0.0)
            out[irrep, :, k * half : (k + 1) * half] = jnp.where(valid, value, 0.0)


def finish(scalars, parts):
    _, column_width, half = parts[0].shape
    vmem = pl.BlockSpec(memory_space=pltpu.VMEM)
    return pl.pallas_call(
        functools.partial(finish_kernel, column_width),
        out_shape=jax.ShapeDtypeStruct((IRREPS, column_width, NC * half), jnp.float32),
        in_specs=[pl.BlockSpec(memory_space=pltpu.SMEM)] + [vmem] * len(parts),
        out_specs=vmem,
        compiler_params=pltpu.CompilerParams(vmem_limit_bytes=4 << 20),
        name="finish",
    )(scalars, *parts)


def local(amplitudes, integrals, irrep_sizes, owner_map):
    pairs, _, slots = amplitudes.shape
    rows, columns = integrals.shape[1:]
    column_width = columns // lax.axis_size("blk")
    plane = NY * NX
    width = columns // plane
    half = pairs // NC
    position = lax.axis_index("blk")
    group = lax.axis_index("grp")
    core = position % NC
    z_part = (position // NC) % NZ

    own = integrals[0]
    near = permute(own, pair_swap)
    middle = permute(own, middle_swap)
    scalars = jnp.concatenate([owner_map, irrep_sizes, jnp.stack([group, position])])
    *split, moved = split_rows(amplitudes, scalars)
    guests = permute(moved, inward)
    passed = permute(middle, outward)
    crossed = permute(near, middle_swap)
    far = permute(crossed[: rows // PARTS], outward)

    matrix = pltpu.VMEM((pairs, slots), jnp.bfloat16)
    slab = pltpu.VMEM((rows, columns), jnp.float32)
    total = pltpu.VMEM((pairs, columns), jnp.float32)
    sems = pltpu.SemaphoreType.DMA((PARTS, 3))
    two_sems = pltpu.SemaphoreType.DMA((2,))
    terms = pairs * columns * slots
    guest_width = moved.shape[1]

    def of(*shape):
        return jax.ShapeDtypeStruct(shape, jnp.float32)

    def other_core(value):
        return permute(value, lambda y, x, z, c, g: (y, x, z, 1 - c, g))

    scratch = [
        pltpu.VMEM((2, rows, columns), jnp.float32),
        pltpu.VMEM((2, pairs, slots), jnp.bfloat16),
        pltpu.VMEM((2, pairs, slots), jnp.bfloat16),
        total,
        pltpu.SemaphoreType.DMA((2, PARTS, 3)),
    ]
    outs = [of(plane, 2 * width, half)] * 2
    kept, sent = call_product(first_kernel, scalars, [own, near], split[:4], [], outs, scratch, 2 * terms)
    first_chip = kept + other_core(sent)
    first = plane_sum(first_chip)

    scratch = [pltpu.VMEM((guest_width, columns), jnp.float32), pltpu.VMEM((pairs, guest_width), jnp.float32), total, two_sems]
    outs = [of(plane, width, half)] * 2
    kept, sent = call_product(
        guest_kernel, scalars, [crossed, guests], [], [], outs, scratch, pairs * columns * guest_width
    )
    guest = staged_sum(kept + other_core(sent), position)
    handed = permute(guest, outward)

    scratch = [slab, matrix, matrix, total, sems, two_sems]
    outs = [of(plane, width, half)] * 2 + [jax.ShapeDtypeStruct((pairs, slots), jnp.bfloat16)] * 2
    kept, sent, *resident = call_product(second_kernel, scalars, [passed, crossed], split[4:], [], outs, scratch, terms)
    got = other_core(sent)
    scratch = [slab, total, pltpu.SemaphoreType.DMA((PARTS,))]
    (result,) = call_product(
        last_kernel,
        scalars,
        [far, middle],
        [],
        [*resident, kept, got],
        [of(plane, width, pairs + half)],
        scratch,
        terms,
    )
    late = plane_sum(result)
    late = late.reshape(width, NC + 1, half).swapaxes(0, 1)
    units = jnp.concatenate([first.reshape(2, width, half), late[NC:], handed[None], late[:NC]], axis=0)
    units = units.reshape(-1, NZ * NC, column_width, half)

    def share(flip):
        here = (z_part * NC + core) ^ flip
        return lax.dynamic_index_in_dim(units, here, 1, keepdims=False)

    parts = [share(0)] + [None] * 3
    for flip in (3, 2, 1):
        parts[flip] = permute(share(flip), lambda y, x, z, c, g: (y, x, z ^ (flip >> 1), c ^ (flip & 1), g))
    return jnp.transpose(finish(scalars, parts), (2, 0, 1))


def solution(mesh):
    in_specs = (P("grp", None, "blk"), P("grp", "blk", None), P(), P())
    out_specs = P("grp", None, "blk")
    return jax.shard_map(local, mesh=mesh, in_specs=in_specs, out_specs=out_specs, check_vma=False)
```

```python
import functools

import jax
import jax.numpy as jnp
from jax import lax
from jax.experimental import pallas as pl
from jax.experimental.pallas import tpu as pltpu
from jax.sharding import PartitionSpec as P


BLOCK = 256
IRREPS = 4
LANES = 128
PARTS = 4
FAR = 2
NY, NX, NZ, NC, NG = 4, 4, 2, 2, 4
AXES = ("blk", "grp")


def blk_index(y, x, z, c):
    return ((y * NX + x) * NZ + z) * NC + c


def every_device():
    for y in range(NY):
        for x in range(NX):
            for z in range(NZ):
                for c in range(NC):
                    for g in range(NG):
                        yield y, x, z, c, g


def permute(value, target):
    pairs = []
    for place in every_device():
        there = target(*place)
        if there is None:
            continue
        pairs.append((blk_index(*place[:4]) * NG + place[4], blk_index(*there[:4]) * NG + there[4]))
    return lax.ppermute(value, AXES, pairs)


def plane_groups():
    return [[blk_index(y, x, z, c) for y in range(NY) for x in range(NX)] for z in range(NZ) for c in range(NC)]


def plane_sum(chip):
    spread = lax.all_to_all(chip, "blk", 0, 0, tiled=True, axis_index_groups=plane_groups())
    return jnp.sum(spread, axis=0)


def pair_swap(y, x, z, c, g):
    return y, x, z, c, g ^ 1


def middle_swap(y, x, z, c, g):
    return (y, x, z, c, 3 - g) if g in (1, 2) else None


def inward(y, x, z, c, g):
    return (y, x, z, c, {0: 1, 3: 2}[g]) if g in (0, 3) else None


def outward(y, x, z, c, g):
    return (y, x, z, c, {1: 0, 2: 3}[g]) if g in (1, 2) else None


def split_kernel(rows, slot_width, scalars, source, *outputs):
    tiles = slot_width // LANES
    group, position = scalars[2 * IRREPS], scalars[2 * IRREPS + 1]
    lane = lax.broadcasted_iota(jnp.int32, (rows, LANES), 1)
    for slot in range(IRREPS):
        irrep = jnp.int32(0)
        for h in range(IRREPS):
            irrep = jnp.where(scalars[h] == (group ^ slot), h, irrep)
        size = scalars[IRREPS + irrep]
        high, low = outputs[2 * slot], outputs[2 * slot + 1]
        for tile in range(tiles):
            first = position * slot_width + tile * LANES
            limit = jnp.where(first // BLOCK < size, size - first % BLOCK, 0)
            value = source[pl.ds(tile * IRREPS + irrep, rows, stride=tiles * IRREPS), :]
            value = jnp.where(lane < limit, value, 0.0)
            rounded = value.astype(jnp.bfloat16)
            place = slice(tile * LANES, (tile + 1) * LANES)
            kept = tiles // FAR
            if slot == IRREPS - 1 and tile >= kept:
                outputs[-1][:, (tile - kept) * LANES : (tile + 1 - kept) * LANES] = value
            high[:, place] = rounded
            low[:, place] = (value - rounded.astype(jnp.float32)).astype(jnp.bfloat16)


def split_rows(amplitudes, scalars):
    pairs, _, slot_width = amplitudes.shape
    rows = 64
    guest_width = slot_width - slot_width // FAR
    view = amplitudes.reshape(pairs, IRREPS, slot_width // LANES, LANES).transpose(0, 2, 1, 3).reshape(-1, LANES)
    return pl.pallas_call(
        functools.partial(split_kernel, rows, slot_width),
        out_shape=[pltpu.HBM((pairs, slot_width), jnp.bfloat16)] * (2 * IRREPS)
        + [pltpu.HBM((pairs, guest_width), jnp.float32)],
        grid_spec=pltpu.PrefetchScalarGridSpec(
            num_scalar_prefetch=1,
            grid=(pairs // rows,),
            in_specs=[pl.BlockSpec((rows * IRREPS * slot_width // LANES, LANES), lambda i, scalars: (i, 0))],
            out_specs=[pl.BlockSpec((rows, slot_width), lambda i, scalars: (i, 0))] * (2 * IRREPS)
            + [pl.BlockSpec((rows, guest_width), lambda i, scalars: (i, 0))],
        ),
        compiler_params=pltpu.CompilerParams(vmem_limit_bytes=16 << 20),
        cost_estimate=pl.CostEstimate(flops=0, bytes_accessed=8 * pairs * IRREPS * slot_width, transcendentals=0),
        name="split_rows",
    )(scalars, *in_hbm([view]))


def halves_of(value):
    rounded = value.astype(jnp.bfloat16)
    return rounded, (value - rounded.astype(jnp.float32)).astype(jnp.bfloat16)


def split_dot(left, right):
    dot = functools.partial(jnp.dot, preferred_element_type=jnp.float32)
    return dot(left[0], right[0]) + (dot(left[0], right[1]) + dot(left[1], right[0]))


def in_hbm(values):
    return [pltpu.with_memory_space_constraint(value, pltpu.HBM) for value in values]


def part_copies(part, sources, here, sems):
    slab, high, low = sources
    slab_here, high_here, low_here = here
    depth = high.shape[1] // PARTS
    place = pl.ds(part * depth, depth)
    return [
        pltpu.make_async_copy(slab.at[place, :], slab_here.at[place, :], sems.at[part, 0]),
        pltpu.make_async_copy(high.at[:, place], high_here.at[:, place], sems.at[part, 1]),
        pltpu.make_async_copy(low.at[:, place], low_here.at[:, place], sems.at[part, 2]),
    ]


def start_parts(parts, sources, here, sems):
    for part in parts:
        for copy in part_copies(part, sources, here, sems):
            copy.start()


def add_parts(parts, sources, here, sems, total):
    slab_here, high_here, low_here = here
    depth = high_here.shape[1] // PARTS
    for part in parts:
        for copy in part_copies(part, sources, here, sems):
            copy.wait()
        place = pl.ds(part * depth, depth)
        term = split_dot((high_here[:, place], low_here[:, place]), halves_of(slab_here[place, :]))
        total[...] = term if part == 0 else total[...] + term


def is_end(scalars):
    group = scalars[2 * IRREPS]
    return (group == 0) | (group == NG - 1)


def put_halves(scalars, total, kept, sent, index):
    groups, _, half = kept.shape
    width = total.shape[1] // groups
    core = scalars[2 * IRREPS + 1] % NC
    for out, which in ((sent, 1 - core), (kept, core)):
        rows = total[pl.ds(pl.multiple_of(which * half, half), half), :]
        out[:, index * width : (index + 1) * width, :] = rows.T.reshape(groups, width, half)


def first_kernel(scalars, own, near, high_0, low_0, high_1, low_1, kept, sent, slabs, highs, lows, total, sems):
    sources = ((own, high_0, low_0), (near, high_1, low_1))
    here = [(slabs.at[k], highs.at[k], lows.at[k]) for k in range(2)]
    for k in range(2):
        start_parts(range(PARTS), sources[k], here[k], sems.at[k])
    for k in range(2):
        add_parts(range(PARTS), sources[k], here[k], sems.at[k], total)
        put_halves(scalars, total, kept, sent, k)


def guest_kernel(scalars, crossed, guests, out, slab, rows, sems):
    depth = rows.shape[1]
    copies = [
        pltpu.make_async_copy(crossed.at[pl.ds(crossed.shape[0] - depth, depth), :], slab, sems.at[0]),
        pltpu.make_async_copy(guests, rows, sems.at[1]),
    ]
    for copy in copies:
        copy.start()
    for copy in copies:
        copy.wait()
    out[...] = split_dot(halves_of(rows[...]), halves_of(slab[...])).T.reshape(out.shape)


def second_kernel(
    scalars, passed, crossed, high, low, high_last, low_last, kept, sent, high_out, low_out, slab, high_here, low_here, total, sems, last_sems
):
    here = (slab, high_here, low_here)
    ends = is_end(scalars)
    pl.when(ends)(lambda: start_parts(range(PARTS), (passed, high, low), here, sems))
    pl.when(jnp.logical_not(ends))(lambda: start_parts(range(PARTS), (crossed, high, low), here, sems))
    copies = [
        pltpu.make_async_copy(high_last, high_out, last_sems.at[0]),
        pltpu.make_async_copy(low_last, low_out, last_sems.at[1]),
    ]
    for copy in copies:
        copy.start()
    add_parts(range(PARTS), (crossed, high, low), here, sems, total)
    put_halves(scalars, total, kept, sent, 0)
    for copy in copies:
        copy.wait()


def last_kernel(scalars, far, middle, high, low, kept, got, out, slab, total, sems):
    ends = is_end(scalars)
    inner = jnp.logical_not(ends)
    depth = far.shape[0]
    pairs = high.shape[0]

    def copy_of(source, part):
        place = pl.ds(part * depth, depth)
        return pltpu.make_async_copy(source.at[place, :], slab.at[place, :], sems.at[part])

    def add(part):
        copy_of(middle, part).wait()
        place = slice(part * depth, (part + 1) * depth)
        term = split_dot((high[:, place], low[:, place]), halves_of(slab[place, :]))
        total[...] = term if part == 0 else total[...] + term

    pl.when(ends)(lambda: copy_of(far, 0).start())

    @pl.when(inner)
    def _():
        for part in range(FAR):
            copy_of(middle, part).start()

    out[:, :, pairs:] = kept[...] + got[...]
    add(0)

    @pl.when(inner)
    def _():
        for part in range(1, FAR):
            add(part)

    out[:, :, :pairs] = total[...].T.reshape(out.shape[0], out.shape[1], pairs)


def call_product(kernel, scalars, moved, fixed, resident, out_shapes, scratch, terms):
    vmem = pl.BlockSpec(memory_space=pltpu.VMEM)
    return pl.pallas_call(
        kernel,
        out_shape=out_shapes,
        in_specs=[pl.BlockSpec(memory_space=pltpu.SMEM)]
        + [pl.BlockSpec(memory_space=pl.ANY)] * (len(moved) + len(fixed))
        + [vmem] * len(resident),
        out_specs=[vmem] * len(out_shapes),
        scratch_shapes=scratch,
        compiler_params=pltpu.CompilerParams(vmem_limit_bytes=16 << 20),
        cost_estimate=pl.CostEstimate(flops=6 * terms, bytes_accessed=6 << 20, transcendentals=0),
    )(scalars, *moved, *in_hbm(fixed), *resident)


def finish_kernel(column_width, scalars, *refs):
    parts, out = refs[:-1], refs[-1]
    half = parts[0].shape[2]
    group, position = scalars[2 * IRREPS], scalars[2 * IRREPS + 1]
    core = position % NC
    column = position * column_width + lax.broadcasted_iota(jnp.int32, parts[0].shape[1:], 0)
    last = IRREPS - 1
    for irrep in range(IRREPS):
        slot = scalars[irrep] ^ group
        size = scalars[IRREPS + irrep]
        valid = (column // BLOCK < size) & (column % BLOCK < size)
        mine = parts[0][slot] + parts[2][slot]
        other = parts[1][slot] + parts[3][slot]
        for k in range(NC):
            whole = (parts[0][last + k] + parts[2][last + k]) + (parts[1][last + k] + parts[3][last + k])
            value = jnp.where(slot == last, whole, jnp.where(core == k, mine, other))
            out[irrep, :, k * half : (k + 1) * half] = jnp.where(valid, value, 0.0)


def finish(scalars, parts):
    _, column_width, half = parts[0].shape
    vmem = pl.BlockSpec(memory_space=pltpu.VMEM)
    return pl.pallas_call(
        functools.partial(finish_kernel, column_width),
        out_shape=jax.ShapeDtypeStruct((IRREPS, column_width, NC * half), jnp.float32),
        in_specs=[pl.BlockSpec(memory_space=pltpu.SMEM)] + [vmem] * len(parts),
        out_specs=vmem,
        compiler_params=pltpu.CompilerParams(vmem_limit_bytes=4 << 20),
        name="finish",
    )(scalars, *parts)


def local(amplitudes, integrals, irrep_sizes, owner_map):
    pairs, _, slots = amplitudes.shape
    rows, columns = integrals.shape[1:]
    column_width = columns // lax.axis_size("blk")
    plane = NY * NX
    width = columns // plane
    half = pairs // NC
    position = lax.axis_index("blk")
    group = lax.axis_index("grp")
    core = position % NC
    z_part = (position // NC) % NZ

    own = integrals[0]
    near = permute(own, pair_swap)
    middle = permute(own, middle_swap)
    scalars = jnp.concatenate([owner_map, irrep_sizes, jnp.stack([group, position])])
    *split, moved = split_rows(amplitudes, scalars)
    guests = permute(moved, inward)
    passed = permute(middle, outward)
    crossed = permute(near, middle_swap)
    far = permute(crossed[: rows // FAR], outward)

    matrix = pltpu.VMEM((pairs, slots), jnp.bfloat16)
    slab = pltpu.VMEM((rows, columns), jnp.float32)
    total = pltpu.VMEM((pairs, columns), jnp.float32)
    sems = pltpu.SemaphoreType.DMA((PARTS, 3))
    two_sems = pltpu.SemaphoreType.DMA((2,))
    terms = pairs * columns * slots
    guest_width = moved.shape[1]

    def of(*shape):
        return jax.ShapeDtypeStruct(shape, jnp.float32)

    def other_core(value):
        return permute(value, lambda y, x, z, c, g: (y, x, z, 1 - c, g))

    scratch = [
        pltpu.VMEM((2, rows, columns), jnp.float32),
        pltpu.VMEM((2, pairs, slots), jnp.bfloat16),
        pltpu.VMEM((2, pairs, slots), jnp.bfloat16),
        total,
        pltpu.SemaphoreType.DMA((2, PARTS, 3)),
    ]
    outs = [of(plane, 2 * width, half)] * 2
    kept, sent = call_product(first_kernel, scalars, [own, near], split[:4], [], outs, scratch, 2 * terms)
    first_chip = kept + other_core(sent)
    first = plane_sum(first_chip)

    scratch = [pltpu.VMEM((guest_width, columns), jnp.float32), pltpu.VMEM((pairs, guest_width), jnp.float32), two_sems]
    outs = [of(plane, width, pairs)]
    (guest,) = call_product(
        guest_kernel, scalars, [crossed, guests], [], [], outs, scratch, pairs * columns * guest_width
    )
    guest = plane_sum(guest)
    handed = permute(guest, outward)

    scratch = [slab, matrix, matrix, total, sems, two_sems]
    outs = [of(plane, width, half)] * 2 + [jax.ShapeDtypeStruct((pairs, slots), jnp.bfloat16)] * 2
    kept, sent, *resident = call_product(second_kernel, scalars, [passed, crossed], split[4:], [], outs, scratch, terms)
    got = other_core(sent)
    scratch = [slab, total, pltpu.SemaphoreType.DMA((FAR,))]
    (result,) = call_product(
        last_kernel,
        scalars,
        [far, middle],
        [],
        [*resident, kept, got],
        [of(plane, width, pairs + half)],
        scratch,
        terms,
    )
    late = plane_sum(result)
    third = (late[:, :pairs] + handed).reshape(width, NC, half).swapaxes(0, 1)
    units = jnp.concatenate([first.reshape(2, width, half), late[None, :, pairs:], third], axis=0)
    units = units.reshape(-1, NZ * NC, column_width, half)

    def share(flip):
        here = (z_part * NC + core) ^ flip
        return lax.dynamic_index_in_dim(units, here, 1, keepdims=False)

    parts = [share(0)] + [None] * 3
    for flip in (3, 2, 1):
        parts[flip] = permute(share(flip), lambda y, x, z, c, g: (y, x, z ^ (flip >> 1), c ^ (flip & 1), g))
    return jnp.transpose(finish(scalars, parts), (2, 0, 1))


def solution(mesh):
    in_specs = (P("grp", None, "blk"), P("grp", "blk", None), P(), P())
    out_specs = P("grp", None, "blk")
    return jax.shard_map(local, mesh=mesh, in_specs=in_specs, out_specs=out_specs, check_vma=False)
```

```python
import functools

import jax
import jax.numpy as jnp
from jax import lax
from jax.experimental import pallas as pl
from jax.experimental.pallas import tpu as pltpu
from jax.sharding import PartitionSpec as P


BLOCK = 256
IRREPS = 4
LANES = 128
PARTS = 4
NY, NX, NZ, NC, NG = 4, 4, 2, 2, 4
AXES = ("blk", "grp")


def blk_index(y, x, z, c):
    return ((y * NX + x) * NZ + z) * NC + c


def every_device():
    for y in range(NY):
        for x in range(NX):
            for z in range(NZ):
                for c in range(NC):
                    for g in range(NG):
                        yield y, x, z, c, g


def permute(value, target):
    pairs = []
    for place in every_device():
        there = target(*place)
        if there is None:
            continue
        pairs.append((blk_index(*place[:4]) * NG + place[4], blk_index(*there[:4]) * NG + there[4]))
    return lax.ppermute(value, AXES, pairs)


def plane_groups():
    return [[blk_index(y, x, z, c) for y in range(NY) for x in range(NX)] for z in range(NZ) for c in range(NC)]


def plane_sum(chip):
    spread = lax.all_to_all(chip, "blk", 0, 0, tiled=True, axis_index_groups=plane_groups())
    return jnp.sum(spread, axis=0)


def pair_swap(y, x, z, c, g):
    return y, x, z, c, g ^ 1


def across(y, x, z, c, g):
    return y, x, z, c, g ^ 2


RELAY = {1: 0, 0: 2, 2: 3, 3: 1}


def relay(y, x, z, c, g):
    return y, x, z, c, RELAY[g]


def split_kernel(rows, slot_width, scalars, source, *outputs):
    tiles = slot_width // LANES
    group, position = scalars[2 * IRREPS], scalars[2 * IRREPS + 1]
    lane = lax.broadcasted_iota(jnp.int32, (rows, LANES), 1)
    for slot in range(IRREPS):
        irrep = jnp.int32(0)
        for h in range(IRREPS):
            irrep = jnp.where(scalars[h] == (group ^ slot), h, irrep)
        size = scalars[IRREPS + irrep]
        high, low = outputs[2 * slot], outputs[2 * slot + 1]
        for tile in range(tiles):
            first = position * slot_width + tile * LANES
            limit = jnp.where(first // BLOCK < size, size - first % BLOCK, 0)
            value = source[pl.ds(tile * IRREPS + irrep, rows, stride=tiles * IRREPS), :]
            value = jnp.where(lane < limit, value, 0.0)
            rounded = value.astype(jnp.bfloat16)
            place = slice(tile * LANES, (tile + 1) * LANES)
            high[:, place] = rounded
            low[:, place] = (value - rounded.astype(jnp.float32)).astype(jnp.bfloat16)


def split_rows(amplitudes, scalars):
    pairs, _, slot_width = amplitudes.shape
    rows = 64
    view = amplitudes.reshape(pairs, IRREPS, slot_width // LANES, LANES).transpose(0, 2, 1, 3).reshape(-1, LANES)
    return pl.pallas_call(
        functools.partial(split_kernel, rows, slot_width),
        out_shape=[pltpu.HBM((pairs, slot_width), jnp.bfloat16)] * (2 * IRREPS),
        grid_spec=pltpu.PrefetchScalarGridSpec(
            num_scalar_prefetch=1,
            grid=(pairs // rows,),
            in_specs=[pl.BlockSpec((rows * IRREPS * slot_width // LANES, LANES), lambda i, scalars: (i, 0))],
            out_specs=[pl.BlockSpec((rows, slot_width), lambda i, scalars: (i, 0))] * (2 * IRREPS),
        ),
        compiler_params=pltpu.CompilerParams(vmem_limit_bytes=16 << 20),
        cost_estimate=pl.CostEstimate(flops=0, bytes_accessed=8 * pairs * IRREPS * slot_width, transcendentals=0),
        name="split_rows",
    )(scalars, *in_hbm([view]))


def halves_of(value):
    rounded = value.astype(jnp.bfloat16)
    return rounded, (value - rounded.astype(jnp.float32)).astype(jnp.bfloat16)


def split_dot(left, right):
    dot = functools.partial(jnp.dot, preferred_element_type=jnp.float32)
    return dot(left[0], right[0]) + (dot(left[0], right[1]) + dot(left[1], right[0]))


def in_hbm(values):
    return [pltpu.with_memory_space_constraint(value, pltpu.HBM) for value in values]


def part_copies(part, sources, here, sems):
    slab, high, low = sources
    slab_here, high_here, low_here = here
    depth = high.shape[1] // PARTS
    place = pl.ds(part * depth, depth)
    return [
        pltpu.make_async_copy(slab.at[place, :], slab_here.at[place, :], sems.at[part, 0]),
        pltpu.make_async_copy(high.at[:, place], high_here.at[:, place], sems.at[part, 1]),
        pltpu.make_async_copy(low.at[:, place], low_here.at[:, place], sems.at[part, 2]),
    ]


def start_parts(parts, sources, here, sems):
    for part in parts:
        for copy in part_copies(part, sources, here, sems):
            copy.start()


def add_parts(parts, sources, here, sems, total):
    slab_here, high_here, low_here = here
    depth = high_here.shape[1] // PARTS
    for part in parts:
        for copy in part_copies(part, sources, here, sems):
            copy.wait()
        place = pl.ds(part * depth, depth)
        term = split_dot((high_here[:, place], low_here[:, place]), halves_of(slab_here[place, :]))
        total[...] = term if part == 0 else total[...] + term


def put_halves(scalars, total, kept, sent, index):
    groups, _, half = kept.shape
    width = total.shape[1] // groups
    core = scalars[2 * IRREPS + 1] % NC
    for out, which in ((sent, 1 - core), (kept, core)):
        rows = total[pl.ds(pl.multiple_of(which * half, half), half), :]
        out[:, index * width : (index + 1) * width, :] = rows.T.reshape(groups, width, half)


def own_kernel(scalars, own, high, low, kept, sent, slab, high_here, low_here, total, sems):
    here = (slab, high_here, low_here)
    start_parts(range(PARTS), (own, high, low), here, sems)
    add_parts(range(PARTS), (own, high, low), here, sems, total)
    put_halves(scalars, total, kept, sent, 0)


def pair_kernel(scalars, one, two, high_1, low_1, high_2, low_2, kept, sent, slabs, highs, lows, total, sems):
    sources = ((one, high_1, low_1), (two, high_2, low_2))
    here = [(slabs.at[k], highs.at[k], lows.at[k]) for k in range(2)]
    for k in range(2):
        start_parts(range(PARTS), sources[k], here[k], sems.at[k])
    for k in range(2):
        add_parts(range(PARTS), sources[k], here[k], sems.at[k], total)
        put_halves(scalars, total, kept, sent, k)


def rows_kernel(scalars, high, low, high_out, low_out, sems):
    depth = high.shape[0] // PARTS
    copies = []
    for part in range(PARTS):
        place = pl.ds(part * depth, depth)
        for k, (there, here) in enumerate(((high, high_out), (low, low_out))):
            copies.append(pltpu.make_async_copy(there.at[place, :], here.at[place, :], sems.at[part, k]))
            copies[-1].start()
    for copy in copies:
        copy.wait()


def last_kernel(scalars, three, high, low, out, slab, total, sems):
    depth = slab.shape[0] // PARTS
    places = [slice(part * depth, (part + 1) * depth) for part in range(PARTS)]
    copies = [
        pltpu.make_async_copy(three.at[pl.ds(part * depth, depth), :], slab.at[pl.ds(part * depth, depth), :], sems.at[part])
        for part in range(PARTS)
    ]
    for copy in copies:
        copy.start()
    for part, place in enumerate(places):
        copies[part].wait()
        term = split_dot((high[:, place], low[:, place]), halves_of(slab[place, :]))
        total[...] = term if part == 0 else total[...] + term
    out[...] = total[...].T.reshape(out.shape)


def call_product(kernel, scalars, moved, fixed, resident, out_shapes, scratch, terms):
    vmem = pl.BlockSpec(memory_space=pltpu.VMEM)
    return pl.pallas_call(
        kernel,
        out_shape=out_shapes,
        in_specs=[pl.BlockSpec(memory_space=pltpu.SMEM)]
        + [pl.BlockSpec(memory_space=pl.ANY)] * (len(moved) + len(fixed))
        + [vmem] * len(resident),
        out_specs=[vmem] * len(out_shapes),
        scratch_shapes=scratch,
        compiler_params=pltpu.CompilerParams(vmem_limit_bytes=16 << 20),
        cost_estimate=pl.CostEstimate(flops=6 * terms, bytes_accessed=6 << 20, transcendentals=0),
    )(scalars, *moved, *in_hbm(fixed), *resident)


def finish_kernel(column_width, scalars, *refs):
    parts, out = refs[:-1], refs[-1]
    half = parts[0].shape[2]
    group, position = scalars[2 * IRREPS], scalars[2 * IRREPS + 1]
    core = position % NC
    column = position * column_width + lax.broadcasted_iota(jnp.int32, parts[0].shape[1:], 0)
    last = IRREPS - 1
    for irrep in range(IRREPS):
        slot = scalars[irrep] ^ group
        size = scalars[IRREPS + irrep]
        valid = (column // BLOCK < size) & (column % BLOCK < size)
        mine = parts[0][slot] + parts[2][slot]
        other = parts[1][slot] + parts[3][slot]
        for k in range(NC):
            whole = (parts[0][last + k] + parts[2][last + k]) + (parts[1][last + k] + parts[3][last + k])
            value = jnp.where(slot == last, whole, jnp.where(core == k, mine, other))
            out[irrep, :, k * half : (k + 1) * half] = jnp.where(valid, value, 0.0)


def finish(scalars, parts):
    _, column_width, half = parts[0].shape
    vmem = pl.BlockSpec(memory_space=pltpu.VMEM)
    return pl.pallas_call(
        functools.partial(finish_kernel, column_width),
        out_shape=jax.ShapeDtypeStruct((IRREPS, column_width, NC * half), jnp.float32),
        in_specs=[pl.BlockSpec(memory_space=pltpu.SMEM)] + [vmem] * len(parts),
        out_specs=vmem,
        compiler_params=pltpu.CompilerParams(vmem_limit_bytes=4 << 20),
        name="finish",
    )(scalars, *parts)


def local(amplitudes, integrals, irrep_sizes, owner_map):
    pairs, _, slots = amplitudes.shape
    rows, columns = integrals.shape[1:]
    column_width = columns // lax.axis_size("blk")
    plane = NY * NX
    width = columns // plane
    half = pairs // NC
    position = lax.axis_index("blk")
    group = lax.axis_index("grp")
    core = position % NC
    z_part = (position // NC) % NZ

    own = integrals[0]
    one = permute(own, pair_swap)
    two = permute(own, across)
    three = permute(jnp.where((group == 0) | (group == NG - 1), one, two), relay)
    scalars = jnp.concatenate([owner_map, irrep_sizes, jnp.stack([group, position])])
    split = split_rows(amplitudes, scalars)

    matrix = pltpu.VMEM((pairs, slots), jnp.bfloat16)
    slab = pltpu.VMEM((rows, columns), jnp.float32)
    total = pltpu.VMEM((pairs, columns), jnp.float32)
    terms = pairs * columns * slots

    def of(*shape):
        return jax.ShapeDtypeStruct(shape, jnp.float32)

    def chip_sum(kept, sent):
        return kept + permute(sent, lambda y, x, z, c, g: (y, x, z, 1 - c, g))

    scratch = [slab, matrix, matrix, total, pltpu.SemaphoreType.DMA((PARTS, 3))]
    outs = [of(plane, width, half)] * 2
    result = call_product(own_kernel, scalars, [own], split[:2], [], outs, scratch, terms)
    chip = chip_sum(*result)
    first = plane_sum(chip)

    scratch = [
        pltpu.VMEM((2, rows, columns), jnp.float32),
        pltpu.VMEM((2, pairs, slots), jnp.bfloat16),
        pltpu.VMEM((2, pairs, slots), jnp.bfloat16),
        total,
        pltpu.SemaphoreType.DMA((2, PARTS, 3)),
    ]
    outs = [of(plane, 2 * width, half)] * 2
    kept, sent = call_product(pair_kernel, scalars, [one, two], split[2:6], [], outs, scratch, 2 * terms)
    chip = chip_sum(kept, sent)
    second = plane_sum(chip)

    outs = [jax.ShapeDtypeStruct((pairs, slots), jnp.bfloat16)] * 2
    scratch = [pltpu.SemaphoreType.DMA((PARTS, 2))]
    resident = call_product(rows_kernel, scalars, [], split[6:], [], outs, scratch, 0)
    scratch = [slab, total, pltpu.SemaphoreType.DMA((PARTS,))]
    outs = [of(plane, width, pairs)]
    (result,) = call_product(last_kernel, scalars, [three], [], resident, outs, scratch, terms)
    third = plane_sum(result)
    third = third.reshape(width, NC, half).swapaxes(0, 1)
    units = jnp.concatenate([first[None], second.reshape(2, width, half), third], axis=0)
    units = units.reshape(-1, NZ * NC, column_width, half)

    def share(flip):
        here = (z_part * NC + core) ^ flip
        return lax.dynamic_index_in_dim(units, here, 1, keepdims=False)

    parts = [share(0)] + [None] * 3
    for flip in (3, 2, 1):
        parts[flip] = permute(share(flip), lambda y, x, z, c, g: (y, x, z ^ (flip >> 1), c ^ (flip & 1), g))
    return jnp.transpose(finish(scalars, parts), (2, 0, 1))


def solution(mesh):
    in_specs = (P("grp", None, "blk"), P("grp", "blk", None), P(), P())
    out_specs = P("grp", None, "blk")
    return jax.shard_map(local, mesh=mesh, in_specs=in_specs, out_specs=out_specs, check_vma=False)
```

```python
import functools

import jax
import jax.numpy as jnp
from jax import lax
from jax.experimental import pallas as pl
from jax.experimental.pallas import tpu as pltpu
from jax.sharding import PartitionSpec as P


BLOCK = 256
IRREPS = 4
LANES = 128
PARTS = 4
NY, NX, NZ, NC, NG = 4, 4, 2, 2, 4
AXES = ("blk", "grp")


def blk_index(y, x, z, c):
    return ((y * NX + x) * NZ + z) * NC + c


def every_device():
    for y in range(NY):
        for x in range(NX):
            for z in range(NZ):
                for c in range(NC):
                    for g in range(NG):
                        yield y, x, z, c, g


def permute(value, target):
    pairs = []
    for place in every_device():
        there = target(*place)
        if there is None:
            continue
        pairs.append((blk_index(*place[:4]) * NG + place[4], blk_index(*there[:4]) * NG + there[4]))
    return lax.ppermute(value, AXES, pairs)


def plane_groups():
    return [[blk_index(y, x, z, c) for y in range(NY) for x in range(NX)] for z in range(NZ) for c in range(NC)]


def plane_sum(chip):
    spread = lax.all_to_all(chip, "blk", 0, 0, tiled=True, axis_index_groups=plane_groups())
    return jnp.sum(spread, axis=0)


def pair_swap(y, x, z, c, g):
    return y, x, z, c, g ^ 1


def across(y, x, z, c, g):
    return y, x, z, c, g ^ 2


RELAY = {1: 0, 0: 2, 2: 3, 3: 1}


def relay(y, x, z, c, g):
    return y, x, z, c, RELAY[g]


def split_kernel(rows, slot_width, scalars, source, *outputs):
    tiles = slot_width // LANES
    group, position = scalars[2 * IRREPS], scalars[2 * IRREPS + 1]
    lane = lax.broadcasted_iota(jnp.int32, (rows, LANES), 1)
    for slot in range(IRREPS):
        irrep = jnp.int32(0)
        for h in range(IRREPS):
            irrep = jnp.where(scalars[h] == (group ^ slot), h, irrep)
        size = scalars[IRREPS + irrep]
        high, low = outputs[2 * slot], outputs[2 * slot + 1]
        for tile in range(tiles):
            first = position * slot_width + tile * LANES
            limit = jnp.where(first // BLOCK < size, size - first % BLOCK, 0)
            value = source[pl.ds(tile * IRREPS + irrep, rows, stride=tiles * IRREPS), :]
            value = jnp.where(lane < limit, value, 0.0)
            rounded = value.astype(jnp.bfloat16)
            place = slice(tile * LANES, (tile + 1) * LANES)
            high[:, place] = rounded
            low[:, place] = (value - rounded.astype(jnp.float32)).astype(jnp.bfloat16)


def split_rows(amplitudes, scalars):
    pairs, _, slot_width = amplitudes.shape
    rows = 64
    view = amplitudes.reshape(pairs, IRREPS, slot_width // LANES, LANES).transpose(0, 2, 1, 3).reshape(-1, LANES)
    return pl.pallas_call(
        functools.partial(split_kernel, rows, slot_width),
        out_shape=[pltpu.HBM((pairs, slot_width), jnp.bfloat16)] * (2 * IRREPS),
        grid_spec=pltpu.PrefetchScalarGridSpec(
            num_scalar_prefetch=1,
            grid=(pairs // rows,),
            in_specs=[pl.BlockSpec((rows * IRREPS * slot_width // LANES, LANES), lambda i, scalars: (i, 0))],
            out_specs=[pl.BlockSpec((rows, slot_width), lambda i, scalars: (i, 0))] * (2 * IRREPS),
        ),
        compiler_params=pltpu.CompilerParams(vmem_limit_bytes=16 << 20),
        cost_estimate=pl.CostEstimate(flops=0, bytes_accessed=8 * pairs * IRREPS * slot_width, transcendentals=0),
        name="split_rows",
    )(scalars, *in_hbm([view]))


def halves_of(value):
    rounded = value.astype(jnp.bfloat16)
    return rounded, (value - rounded.astype(jnp.float32)).astype(jnp.bfloat16)


def split_dot(left, right):
    dot = functools.partial(jnp.dot, preferred_element_type=jnp.float32)
    return dot(left[0], right[0]) + (dot(left[0], right[1]) + dot(left[1], right[0]))


def in_hbm(values):
    return [pltpu.with_memory_space_constraint(value, pltpu.HBM) for value in values]


def part_copies(part, sources, here, sems):
    slab, high, low = sources
    slab_here, high_here, low_here = here
    depth = high.shape[1] // PARTS
    place = pl.ds(part * depth, depth)
    return [
        pltpu.make_async_copy(slab.at[place, :], slab_here.at[place, :], sems.at[part, 0]),
        pltpu.make_async_copy(high.at[:, place], high_here.at[:, place], sems.at[part, 1]),
        pltpu.make_async_copy(low.at[:, place], low_here.at[:, place], sems.at[part, 2]),
    ]


def start_parts(parts, sources, here, sems):
    for part in parts:
        for copy in part_copies(part, sources, here, sems):
            copy.start()


def add_parts(parts, sources, here, sems, total):
    slab_here, high_here, low_here = here
    depth = high_here.shape[1] // PARTS
    for part in parts:
        for copy in part_copies(part, sources, here, sems):
            copy.wait()
        place = pl.ds(part * depth, depth)
        term = split_dot((high_here[:, place], low_here[:, place]), halves_of(slab_here[place, :]))
        total[...] = term if part == 0 else total[...] + term


def put_halves(scalars, total, kept, sent, index):
    groups, _, half = kept.shape
    width = total.shape[1] // groups
    core = scalars[2 * IRREPS + 1] % NC
    for out, which in ((sent, 1 - core), (kept, core)):
        rows = total[pl.ds(pl.multiple_of(which * half, half), half), :]
        out[:, index * width : (index + 1) * width, :] = rows.T.reshape(groups, width, half)


def own_kernel(scalars, own, high, low, kept, sent, slab, high_here, low_here, total, sems):
    here = (slab, high_here, low_here)
    start_parts(range(PARTS), (own, high, low), here, sems)
    add_parts(range(PARTS), (own, high, low), here, sems, total)
    put_halves(scalars, total, kept, sent, 0)


def pair_kernel(scalars, one, two, high_1, low_1, high_2, low_2, kept, sent, total):
    for k, (slab, high, low) in enumerate(((one, high_1, low_1), (two, high_2, low_2))):
        total[...] = split_dot((high[...], low[...]), halves_of(slab[...]))
        put_halves(scalars, total, kept, sent, k)


def rows_kernel(scalars, *refs):
    count = (len(refs) - 1) // 2
    there, here, sems = refs[:count], refs[count:-1], refs[-1]
    depth = there[0].shape[0] // PARTS
    copies = []
    for k in range(count):
        for part in range(PARTS):
            place = pl.ds(part * depth, depth)
            copies.append(pltpu.make_async_copy(there[k].at[place, :], here[k].at[place, :], sems.at[k, part]))
            copies[-1].start()
    for copy in copies:
        copy.wait()


def last_kernel(scalars, three, high, low, out):
    out[...] = split_dot((high[...], low[...]), halves_of(three[...])).T.reshape(out.shape)


def call_product(kernel, scalars, moved, fixed, resident, out_shapes, scratch, terms):
    vmem = pl.BlockSpec(memory_space=pltpu.VMEM)
    return pl.pallas_call(
        kernel,
        out_shape=out_shapes,
        in_specs=[pl.BlockSpec(memory_space=pltpu.SMEM)]
        + [pl.BlockSpec(memory_space=pl.ANY)] * (len(moved) + len(fixed))
        + [vmem] * len(resident),
        out_specs=[vmem] * len(out_shapes),
        scratch_shapes=scratch,
        compiler_params=pltpu.CompilerParams(vmem_limit_bytes=16 << 20),
        cost_estimate=pl.CostEstimate(flops=6 * terms, bytes_accessed=6 << 20, transcendentals=0),
    )(scalars, *moved, *in_hbm(fixed), *resident)


def finish_kernel(column_width, scalars, *refs):
    parts, out = refs[:-1], refs[-1]
    half = parts[0].shape[2]
    group, position = scalars[2 * IRREPS], scalars[2 * IRREPS + 1]
    core = position % NC
    column = position * column_width + lax.broadcasted_iota(jnp.int32, parts[0].shape[1:], 0)
    last = IRREPS - 1
    for irrep in range(IRREPS):
        slot = scalars[irrep] ^ group
        size = scalars[IRREPS + irrep]
        valid = (column // BLOCK < size) & (column % BLOCK < size)
        mine, other = parts[0][slot], parts[1][slot]
        for k in range(NC):
            whole = parts[0][last + k] + parts[1][last + k]
            value = jnp.where(slot == last, whole, jnp.where(core == k, mine, other))
            out[irrep, :, k * half : (k + 1) * half] = jnp.where(valid, value, 0.0)


def finish(scalars, parts):
    _, column_width, half = parts[0].shape
    vmem = pl.BlockSpec(memory_space=pltpu.VMEM)
    return pl.pallas_call(
        functools.partial(finish_kernel, column_width),
        out_shape=jax.ShapeDtypeStruct((IRREPS, column_width, NC * half), jnp.float32),
        in_specs=[pl.BlockSpec(memory_space=pltpu.SMEM)] + [vmem] * len(parts),
        out_specs=vmem,
        compiler_params=pltpu.CompilerParams(vmem_limit_bytes=4 << 20),
        name="finish",
    )(scalars, *parts)


def local(amplitudes, integrals, irrep_sizes, owner_map):
    pairs, _, slots = amplitudes.shape
    rows, columns = integrals.shape[1:]
    column_width = columns // lax.axis_size("blk")
    plane = NY * NX
    width = columns // plane
    half = pairs // NC
    position = lax.axis_index("blk")
    group = lax.axis_index("grp")
    core = position % NC
    z_part = (position // NC) % NZ

    own = integrals[0]
    one = permute(own, pair_swap)
    two = permute(own, across)
    three = permute(jnp.where((group == 0) | (group == NG - 1), one, two), relay)
    scalars = jnp.concatenate([owner_map, irrep_sizes, jnp.stack([group, position])])
    split = split_rows(amplitudes, scalars)

    matrix = pltpu.VMEM((pairs, slots), jnp.bfloat16)
    slab = pltpu.VMEM((rows, columns), jnp.float32)
    total = pltpu.VMEM((pairs, columns), jnp.float32)
    terms = pairs * columns * slots

    def of(*shape):
        return jax.ShapeDtypeStruct(shape, jnp.float32)

    def chip_sum(kept, sent):
        return kept + permute(sent, lambda y, x, z, c, g: (y, x, z, 1 - c, g))

    scratch = [slab, matrix, matrix, total, pltpu.SemaphoreType.DMA((PARTS, 3))]
    outs = [of(plane, width, half)] * 2
    result = call_product(own_kernel, scalars, [own], split[:2], [], outs, scratch, terms)
    chip = chip_sum(*result)
    first = plane_sum(chip)

    def brought(values):
        outs = [jax.ShapeDtypeStruct((pairs, slots), jnp.bfloat16)] * len(values)
        scratch = [pltpu.SemaphoreType.DMA((len(values), PARTS))]
        return call_product(rows_kernel, scalars, [], values, [], outs, scratch, 0)

    resident = brought(split[2:6])
    outs = [of(plane, 2 * width, half)] * 2
    kept, sent = call_product(pair_kernel, scalars, [], [], [one, two, *resident], outs, [total], 2 * terms)
    chip = chip_sum(kept, sent)
    second = plane_sum(chip)

    resident = brought(split[6:])
    outs = [of(plane, width, pairs)]
    (result,) = call_product(last_kernel, scalars, [], [], [three, *resident], outs, [], terms)
    third = plane_sum(result)
    third = third.reshape(width, NC, half).swapaxes(0, 1)
    units = jnp.concatenate([first[None], second.reshape(2, width, half), third], axis=0)
    units = units.reshape(-1, NZ, NC * column_width, half)
    here = lax.dynamic_index_in_dim(units, z_part, 1, keepdims=False)
    there = lax.dynamic_index_in_dim(units, 1 - z_part, 1, keepdims=False)
    units = here + permute(there, lambda y, x, z, c, g: (y, x, 1 - z, c, g))
    units = units.reshape(-1, NC, column_width, half)
    here = lax.dynamic_index_in_dim(units, core, 1, keepdims=False)
    there = lax.dynamic_index_in_dim(units, 1 - core, 1, keepdims=False)
    parts = [here, permute(there, lambda y, x, z, c, g: (y, x, z, 1 - c, g))]
    return jnp.transpose(finish(scalars, parts), (2, 0, 1))


def solution(mesh):
    in_specs = (P("grp", None, "blk"), P("grp", "blk", None), P(), P())
    out_specs = P("grp", None, "blk")
    return jax.shard_map(local, mesh=mesh, in_specs=in_specs, out_specs=out_specs, check_vma=False)
```

```python
import functools

import jax
import jax.numpy as jnp
from jax import lax
from jax.experimental import pallas as pl
from jax.experimental.pallas import tpu as pltpu
from jax.sharding import PartitionSpec as P


BLOCK = 256
IRREPS = 4
LANES = 128
PARTS = 4
NY, NX, NZ, NC, NG = 4, 4, 2, 2, 4
AXES = ("blk", "grp")


def blk_index(y, x, z, c):
    return ((y * NX + x) * NZ + z) * NC + c


def every_device():
    for y in range(NY):
        for x in range(NX):
            for z in range(NZ):
                for c in range(NC):
                    for g in range(NG):
                        yield y, x, z, c, g


def permute(value, target):
    pairs = []
    for place in every_device():
        there = target(*place)
        if there is None:
            continue
        pairs.append((blk_index(*place[:4]) * NG + place[4], blk_index(*there[:4]) * NG + there[4]))
    return lax.ppermute(value, AXES, pairs)


def plane_groups():
    return [[blk_index(y, x, z, c) for y in range(NY) for x in range(NX)] for z in range(NZ) for c in range(NC)]


def plane_sum(chip):
    spread = lax.all_to_all(chip, "blk", 0, 0, tiled=True, axis_index_groups=plane_groups())
    return jnp.sum(spread, axis=0)


def box_sum(chip):
    groups = [[blk_index(y, x, z, c) for y in range(NY) for x in range(NX) for z in range(NZ)] for c in range(NC)]
    spread = lax.all_to_all(chip, "blk", 0, 0, tiled=True, axis_index_groups=groups)
    return jnp.sum(spread, axis=0)


def pair_swap(y, x, z, c, g):
    return y, x, z, c, g ^ 1


def across(y, x, z, c, g):
    return y, x, z, c, g ^ 2


RELAY = {1: 0, 0: 2, 2: 3, 3: 1}


def relay(y, x, z, c, g):
    return y, x, z, c, RELAY[g]


def split_kernel(rows, slot_width, scalars, source, *outputs):
    tiles = slot_width // LANES
    group, position = scalars[2 * IRREPS], scalars[2 * IRREPS + 1]
    lane = lax.broadcasted_iota(jnp.int32, (rows, LANES), 1)
    for slot in range(IRREPS):
        irrep = jnp.int32(0)
        for h in range(IRREPS):
            irrep = jnp.where(scalars[h] == (group ^ slot), h, irrep)
        size = scalars[IRREPS + irrep]
        high, low = outputs[2 * slot], outputs[2 * slot + 1]
        for tile in range(tiles):
            first = position * slot_width + tile * LANES
            limit = jnp.where(first // BLOCK < size, size - first % BLOCK, 0)
            value = source[pl.ds(tile * IRREPS + irrep, rows, stride=tiles * IRREPS), :]
            value = jnp.where(lane < limit, value, 0.0)
            rounded = value.astype(jnp.bfloat16)
            place = slice(tile * LANES, (tile + 1) * LANES)
            high[:, place] = rounded
            low[:, place] = (value - rounded.astype(jnp.float32)).astype(jnp.bfloat16)


def split_rows(amplitudes, scalars):
    pairs, _, slot_width = amplitudes.shape
    rows = 64
    view = amplitudes.reshape(pairs, IRREPS, slot_width // LANES, LANES).transpose(0, 2, 1, 3).reshape(-1, LANES)
    return pl.pallas_call(
        functools.partial(split_kernel, rows, slot_width),
        out_shape=[pltpu.HBM((pairs, slot_width), jnp.bfloat16)] * (2 * IRREPS),
        grid_spec=pltpu.PrefetchScalarGridSpec(
            num_scalar_prefetch=1,
            grid=(pairs // rows,),
            in_specs=[pl.BlockSpec((rows * IRREPS * slot_width // LANES, LANES), lambda i, scalars: (i, 0))],
            out_specs=[pl.BlockSpec((rows, slot_width), lambda i, scalars: (i, 0))] * (2 * IRREPS),
        ),
        compiler_params=pltpu.CompilerParams(vmem_limit_bytes=16 << 20),
        cost_estimate=pl.CostEstimate(flops=0, bytes_accessed=8 * pairs * IRREPS * slot_width, transcendentals=0),
        name="split_rows",
    )(scalars, *in_hbm([view]))


def halves_of(value):
    rounded = value.astype(jnp.bfloat16)
    return rounded, (value - rounded.astype(jnp.float32)).astype(jnp.bfloat16)


def split_dot(left, right):
    dot = functools.partial(jnp.dot, preferred_element_type=jnp.float32)
    return dot(left[0], right[0]) + (dot(left[0], right[1]) + dot(left[1], right[0]))


def in_hbm(values):
    return [pltpu.with_memory_space_constraint(value, pltpu.HBM) for value in values]


def part_copies(part, sources, here, sems):
    slab, high, low = sources
    slab_here, high_here, low_here = here
    depth = high.shape[1] // PARTS
    place = pl.ds(part * depth, depth)
    return [
        pltpu.make_async_copy(slab.at[place, :], slab_here.at[place, :], sems.at[part, 0]),
        pltpu.make_async_copy(high.at[:, place], high_here.at[:, place], sems.at[part, 1]),
        pltpu.make_async_copy(low.at[:, place], low_here.at[:, place], sems.at[part, 2]),
    ]


def start_parts(parts, sources, here, sems):
    for part in parts:
        for copy in part_copies(part, sources, here, sems):
            copy.start()


def add_parts(parts, sources, here, sems, total):
    slab_here, high_here, low_here = here
    depth = high_here.shape[1] // PARTS
    for part in parts:
        for copy in part_copies(part, sources, here, sems):
            copy.wait()
        place = pl.ds(part * depth, depth)
        term = split_dot((high_here[:, place], low_here[:, place]), halves_of(slab_here[place, :]))
        total[...] = term if part == 0 else total[...] + term


def put_halves(scalars, total, kept, sent, index):
    groups, _, half = kept.shape
    width = total.shape[1] // groups
    core = scalars[2 * IRREPS + 1] % NC
    for out, which in ((sent, 1 - core), (kept, core)):
        rows = total[pl.ds(pl.multiple_of(which * half, half), half), :]
        out[:, index * width : (index + 1) * width, :] = rows.T.reshape(groups, width, half)


def own_kernel(scalars, own, high, low, kept, sent, slab, high_here, low_here, total, sems):
    here = (slab, high_here, low_here)
    start_parts(range(PARTS), (own, high, low), here, sems)
    add_parts(range(PARTS), (own, high, low), here, sems, total)
    put_halves(scalars, total, kept, sent, 0)


def pair_kernel(scalars, one, two, high_1, low_1, high_2, low_2, kept, sent, total):
    for k, (slab, high, low) in enumerate(((one, high_1, low_1), (two, high_2, low_2))):
        total[...] = split_dot((high[...], low[...]), halves_of(slab[...]))
        put_halves(scalars, total, kept, sent, k)


def rows_kernel(scalars, *refs):
    count = (len(refs) - 1) // 2
    there, here, sems = refs[:count], refs[count:-1], refs[-1]
    depth = there[0].shape[0] // PARTS
    copies = []
    for k in range(count):
        for part in range(PARTS):
            place = pl.ds(part * depth, depth)
            copies.append(pltpu.make_async_copy(there[k].at[place, :], here[k].at[place, :], sems.at[k, part]))
            copies[-1].start()
    for copy in copies:
        copy.wait()


def last_kernel(scalars, three, high, low, out):
    out[...] = split_dot((high[...], low[...]), halves_of(three[...])).T.reshape(out.shape)


def call_product(kernel, scalars, moved, fixed, resident, out_shapes, scratch, terms):
    vmem = pl.BlockSpec(memory_space=pltpu.VMEM)
    return pl.pallas_call(
        kernel,
        out_shape=out_shapes,
        in_specs=[pl.BlockSpec(memory_space=pltpu.SMEM)]
        + [pl.BlockSpec(memory_space=pl.ANY)] * (len(moved) + len(fixed))
        + [vmem] * len(resident),
        out_specs=[vmem] * len(out_shapes),
        scratch_shapes=scratch,
        compiler_params=pltpu.CompilerParams(vmem_limit_bytes=16 << 20),
        cost_estimate=pl.CostEstimate(flops=6 * terms, bytes_accessed=6 << 20, transcendentals=0),
    )(scalars, *moved, *in_hbm(fixed), *resident)


def finish_kernel(column_width, scalars, *refs):
    parts, out = refs[:-1], refs[-1]
    half = parts[0].shape[2]
    group, position = scalars[2 * IRREPS], scalars[2 * IRREPS + 1]
    core = position % NC
    column = position * column_width + lax.broadcasted_iota(jnp.int32, parts[0].shape[1:], 0)
    last = IRREPS - 1
    for irrep in range(IRREPS):
        slot = scalars[irrep] ^ group
        size = scalars[IRREPS + irrep]
        valid = (column // BLOCK < size) & (column % BLOCK < size)
        mine, other = parts[0][slot], parts[1][slot]
        for k in range(NC):
            whole = parts[0][last + k] + parts[1][last + k]
            value = jnp.where(slot == last, whole, jnp.where(core == k, mine, other))
            out[irrep, :, k * half : (k + 1) * half] = jnp.where(valid, value, 0.0)


def finish(scalars, parts):
    _, column_width, half = parts[0].shape
    vmem = pl.BlockSpec(memory_space=pltpu.VMEM)
    return pl.pallas_call(
        functools.partial(finish_kernel, column_width),
        out_shape=jax.ShapeDtypeStruct((IRREPS, column_width, NC * half), jnp.float32),
        in_specs=[pl.BlockSpec(memory_space=pltpu.SMEM)] + [vmem] * len(parts),
        out_specs=vmem,
        compiler_params=pltpu.CompilerParams(vmem_limit_bytes=4 << 20),
        name="finish",
    )(scalars, *parts)


def local(amplitudes, integrals, irrep_sizes, owner_map):
    pairs, _, slots = amplitudes.shape
    rows, columns = integrals.shape[1:]
    column_width = columns // lax.axis_size("blk")
    plane = NY * NX
    width = columns // plane
    half = pairs // NC
    position = lax.axis_index("blk")
    group = lax.axis_index("grp")
    core = position % NC
    z_part = (position // NC) % NZ

    own = integrals[0]
    one = permute(own, pair_swap)
    two = permute(own, across)
    three = permute(jnp.where((group == 0) | (group == NG - 1), one, two), relay)
    scalars = jnp.concatenate([owner_map, irrep_sizes, jnp.stack([group, position])])
    split = split_rows(amplitudes, scalars)

    matrix = pltpu.VMEM((pairs, slots), jnp.bfloat16)
    slab = pltpu.VMEM((rows, columns), jnp.float32)
    total = pltpu.VMEM((pairs, columns), jnp.float32)
    terms = pairs * columns * slots

    def of(*shape):
        return jax.ShapeDtypeStruct(shape, jnp.float32)

    def chip_sum(kept, sent):
        return kept + permute(sent, lambda y, x, z, c, g: (y, x, z, 1 - c, g))

    scratch = [slab, matrix, matrix, total, pltpu.SemaphoreType.DMA((PARTS, 3))]
    outs = [of(plane, width, half)] * 2
    result = call_product(own_kernel, scalars, [own], split[:2], [], outs, scratch, terms)
    chip = chip_sum(*result)
    first = plane_sum(chip)

    def brought(values):
        outs = [jax.ShapeDtypeStruct((pairs, slots), jnp.bfloat16)] * len(values)
        scratch = [pltpu.SemaphoreType.DMA((len(values), PARTS))]
        return call_product(rows_kernel, scalars, [], values, [], outs, scratch, 0)

    resident = brought(split[2:6])
    outs = [of(plane, 2 * width, half)] * 2
    kept, sent = call_product(pair_kernel, scalars, [], [], [one, two, *resident], outs, [total], 2 * terms)
    chip = chip_sum(kept, sent)
    second = plane_sum(chip)

    resident = brought(split[6:])
    outs = [of(plane, width, pairs)]
    (result,) = call_product(last_kernel, scalars, [], [], [three, *resident], outs, [], terms)
    third = box_sum(result.reshape(plane * NZ, width // NZ, pairs))
    third = third.reshape(width // NZ, NC, half).swapaxes(0, 1)
    early = jnp.concatenate([first[None], second.reshape(2, width, half)], axis=0)
    early = early.reshape(-1, NZ, NC * column_width, half)
    here = lax.dynamic_index_in_dim(early, z_part, 1, keepdims=False)
    there = lax.dynamic_index_in_dim(early, 1 - z_part, 1, keepdims=False)
    early = here + permute(there, lambda y, x, z, c, g: (y, x, 1 - z, c, g))
    units = jnp.concatenate([early, third], axis=0)
    units = units.reshape(-1, NC, column_width, half)
    here = lax.dynamic_index_in_dim(units, core, 1, keepdims=False)
    there = lax.dynamic_index_in_dim(units, 1 - core, 1, keepdims=False)
    parts = [here, permute(there, lambda y, x, z, c, g: (y, x, z, 1 - c, g))]
    return jnp.transpose(finish(scalars, parts), (2, 0, 1))


def solution(mesh):
    in_specs = (P("grp", None, "blk"), P("grp", "blk", None), P(), P())
    out_specs = P("grp", None, "blk")
    return jax.shard_map(local, mesh=mesh, in_specs=in_specs, out_specs=out_specs, check_vma=False)
```
